32 devices in a mesh: member: 4 (over z), space: 8 (over y, x, core).
Axes of the slice: x: 2, y: 2, z: 4, core: 2. Of those that a mesh axis runs over, the one named last changes fastest.
Arguments:
- particles: float32 [32, 2, 200, 800], P('member', None, 'space'), may hold values from -8 to 8
- loglik_grad: float32 [32, 2, 200, 800], P('member', None, 'space'), may hold values from -0.00036621094 to 0.00036621094
- wave_prev: float32 [32, 2, 200, 800], P('member', None, 'space'), may hold values from -6 to 6
- wave_now: float32 [32, 2, 200, 800], P('member', None, 'space'), may hold values from -6 to 6
- ghosts: float32 [32, 8, 200, 800], P('member', None, 'space'), may hold values from -6 to 6
- src_cell: int32 [32], P('member'), may hold values from 0 to 159999
Outputs:
- new_particles: float32 [32, 2, 200, 800], P('member', None, 'space')
- wave_before: float32 [32, 2, 200, 800], P('member', None, 'space')
- wave_after: float32 [32, 2, 200, 800], P('member', None, 'space')
The draws below stay inside these ranges and needn't reach their ends.
Inputs may be any that keep to these rules, and one draw needn't show every extreme that they name: `src_cell`: the flat index 800 * x + y of each particle's source cell on depth plane 0.
All inputs are finite; a program needn't handle non-finite values.
Results may differ from the reference program's by a relative error of at most 0.0003.
Values sent between devices are 32-bit elements; how exact they have to be, the bound alone decides.
No kernel may reach another device: no remote copies, remote signals or barrier semaphores. Data moves between devices by JAX's collectives and lax.ppermute only.
A program may use at most 128 MiB of HBM per device.

```python
import math
import jax
import jax.numpy as jnp
from jax import lax

CX = 25
NY = 800
NZ = 2
GHOST = 4
STEPS = 4
PARTICLES = 32
NX = 200


def draw_particles(key, part):
    base_key = jax.random.fold_in(key, 11)
    scale_key, block_key, value_key = jax.random.split(base_key, 3)
    shape = (PARTICLES, NZ, NX, NY)
    blocks = NX // CX
    scales = jnp.exp(jax.random.uniform(scale_key, (PARTICLES, 1, 1, 1), jnp.float32, math.log(0.5), math.log(2.0)))
    block_scales = jnp.exp(jax.random.uniform(block_key, (PARTICLES, 1, blocks, 1), jnp.float32, -0.7, 0.7))
    spread = scales * jnp.repeat(block_scales, CX, axis=2)
    values = jnp.clip(jax.random.normal(value_key, shape, jnp.float32), -4.0, 4.0)
    result = spread * values
    return jnp.clip(result, -8.0, 8.0)


def plant(entries, rng, smallest, top_value):
    dims = entries.shape
    place = [jax.random.randint(jax.random.fold_in(rng, axis), (), 0, dims[axis]) for axis in range(len(dims))]
    entries = entries.at[tuple(place)].set(smallest)
    longest = dims.index(max(dims))
    place[longest] = (place[longest] + 1) % dims[longest]
    return entries.at[tuple(place)].set(top_value)


def block_scale(own_key, shape, cuts, smallest, top_value):
    def one(position, blocks):
        heights = jax.random.uniform(jax.random.fold_in(jax.random.fold_in(own_key, 6), position), (blocks,), jnp.float32, smallest / len(cuts), top_value / len(cuts))
        return jnp.repeat(jnp.exp(heights), shape[position] // blocks).reshape((-1,) + (1,) * (len(shape) - position - 1))

    loudness = one(*cuts[0])
    for cut in cuts[1:]:
        loudness = loudness * one(*cut)
    return loudness


def noise(rng, dims, scale, reach, cuts=(), held_as=jnp.bfloat16):
    array = scale * jax.random.normal(rng, dims, jnp.float32)
    if cuts:
        array = array * block_scale(rng, dims, cuts, -0.22, 0.18)
    return jnp.clip(array, -reach, reach).astype(held_as)


def setup_inputs(seed: int = 0) -> dict:
    splits = jax.random.split(jax.random.key(seed), 7)
    return {
        "particles": draw_particles(jax.random.fold_in(splits[6], 71), 0),
        "loglik_grad": noise(splits[1], (PARTICLES, NZ, NX, NY), (8.0 / (NX * NY * NZ)), 0.00036621094, ((0, 4), (2, 8)), jnp.float32),
        "wave_prev": noise(splits[2], (PARTICLES, NZ, NX, NY), 1.0, 6.0, ((0, 4), (2, 8)), jnp.float32),
        "wave_now": noise(splits[3], (PARTICLES, NZ, NX, NY), 1.0, 6.0, ((0, 4), (2, 8)), jnp.float32),
        "ghosts": noise(splits[4], (PARTICLES, 2 * GHOST, NX, NY), 1.0, 6.0, ((0, 4), (2, 8)), jnp.float32),
        "src_cell": plant(jax.random.randint(splits[5], (PARTICLES,), 0, NX * NY), jax.random.fold_in(splits[5], 1), 0, (NX * NY) - 1).astype(jnp.int32),
    }


weights = (-205.0 / 72.0, 8.0 / 5.0, -1.0 / 5.0, 8.0 / 315.0, -1.0 / 560.0)
step_size = 0.25
courant = 0.3


def laplace(wide, top, bottom):
    extent = wide.shape[-2] - 8
    center = wide[..., 4:4 + extent, :]
    depth = center.shape[-3]
    across = center.shape[-1]
    pad_spec = [(0, 0)] * (center.ndim - 1) + [(4, 4)]
    ypad = jnp.pad(center, pad_spec)
    column = jnp.concatenate([top, center, bottom], axis=-3)
    total = (3.0 * weights[0]) * center
    for offset in range(1, 5):
        total = total + weights[offset] * (wide[..., 4 + offset:4 + offset + extent, :] + wide[..., 4 - offset:4 - offset + extent, :])
        total = total + weights[offset] * (ypad[..., 4 + offset:4 + offset + across] + ypad[..., 4 - offset:4 - offset + across])
        total = total + weights[offset] * (column[..., 4 + offset:4 + offset + depth, :, :] + column[..., 4 - offset:4 - offset + depth, :, :])
    return total


def reference(particles, loglik_grad, wave_prev, wave_now, ghosts, src_cell):
    count = particles.shape[0]
    flat = particles.reshape(count, -1)
    gflat = loglik_grad.reshape(count, -1)

    def one_row(single):
        return jnp.sum(jnp.square(flat - single[None, :]), axis=1)

    dist = lax.map(one_row, flat)
    offdiag = 1.0 - jnp.eye(count, dtype=jnp.float32)
    band = jnp.sum(dist * offdiag) / (count * (count - 1) * math.log(count + 1))
    kern = jnp.exp(-dist / band)
    kernel_grad = jnp.dot(kern, gflat, precision=lax.Precision.HIGHEST, preferred_element_type=jnp.float32)
    kernel_pos = jnp.dot(kern, flat, precision=lax.Precision.HIGHEST, preferred_element_type=jnp.float32)
    moved = flat + step_size * ((0.5 * band) * kernel_grad + jnp.sum(kern, axis=1)[:, None] * flat - kernel_pos)
    new_particles = moved.reshape(particles.shape)

    coef = jnp.square(courant * (1.0 + 0.3 * jnp.tanh(particles)))

    def propagate(items):
        prev, now, ghost, factor, source = items
        src_x = source // NY
        src_y = source % NY
        xs = jnp.arange(NX, dtype=jnp.int32)
        ys = jnp.arange(NY, dtype=jnp.int32)
        spot = ((xs[:, None] == src_x) & (ys[None, :] == src_y)).astype(jnp.float32)
        plane = (jnp.arange(NZ, dtype=jnp.int32) == 0).astype(jnp.float32)
        inject = plane[:, None, None] * spot[None, :, :]
        top = ghost[:GHOST]
        bottom = ghost[GHOST:]
        for step in range(STEPS):
            wide = jnp.pad(now, ((0, 0), (4, 4), (0, 0)))
            amplitude = 2.0 * math.cos(1.3 * step)
            following = 2.0 * now - prev + factor * laplace(wide, top, bottom) + amplitude * inject
            prev, now = now, following
        return prev, now

    wave_before, wave_after = lax.map(propagate, (wave_prev, wave_now, ghosts, coef, src_cell))
    return new_particles, wave_before, wave_after
```

```python
import functools
import math

import jax
import jax.numpy as jnp
from jax import lax
from jax.experimental import pallas as pl
from jax.experimental.pallas import tpu as pltpu
from jax.sharding import PartitionSpec as P

GHOST = 4
STEPS = 4
LANES = 128

weights = (-205.0 / 72.0, 8.0 / 5.0, -1.0 / 5.0, 8.0 / 315.0, -1.0 / 560.0)
step_size = 0.25
courant = 0.3

VMEM = pl.BlockSpec(memory_space=pltpu.VMEM)
SMEM = pl.BlockSpec(memory_space=pltpu.SMEM)


def params():
    return pltpu.CompilerParams(vmem_limit_bytes=40 << 20)


class Packing:
    def __init__(self, width, depth, across, members):
        self.width, self.depth, self.across, self.members = width, depth, across, members
        self.rows = width * depth
        self.full = across // LANES
        self.tail = across % LANES
        self.group = LANES // self.tail if self.tail else 1
        self.tail_tiles = -(-self.rows // self.group) if self.tail else 0
        total = self.rows * self.full + self.tail_tiles
        self.tiles = -(-total // members)
        self.lanes = self.tiles * LANES
        self.spare = self.tiles * members - total

    def runs(self, row):
        tile, at, left = row * self.full, 0, self.full
        while left:
            chunk, place = divmod(tile, self.tiles)
            count = min(left, self.tiles - place)
            yield chunk, place * LANES, at * LANES, count * LANES
            tile, at, left = tile + count, at + count, left - count

    def tail_place(self, index):
        chunk, place = divmod(self.rows * self.full + index, self.tiles)
        return chunk, place * LANES


def pack_body(pack, cuts, me_ref, cells_ref, *refs):
    outs, buf = refs[:-1], refs[-1]
    own = cells_ref.shape[2]
    me = me_ref[0]
    slots = [lax.rem(chunk - me + pack.members, pack.members) for chunk in range(pack.members)]
    for row in range(pack.rows):
        x, z = divmod(row, pack.depth)
        for chunk, there, here, count in pack.runs(row):
            buf[slots[chunk], :, there : there + count] = cells_ref[x, z, :, here : here + count]
    start = pack.full * LANES
    for index in range(pack.tail_tiles):
        chunk, place = pack.tail_place(index)
        pieces = []
        for row in range(index * pack.group, min(pack.rows, (index + 1) * pack.group)):
            x, z = divmod(row, pack.depth)
            pieces.append(cells_ref[x, z, :, start : start + pack.tail])
        empty = LANES - pack.tail * len(pieces)
        if empty:
            pieces.append(jnp.zeros((own, empty), jnp.float32))
        buf[slots[chunk], :, place : place + LANES] = jnp.concatenate(pieces, axis=1)
    for index in range(pack.spare):
        chunk, place = pack.tail_place(pack.tail_tiles + index)
        buf[slots[chunk], :, place : place + LANES] = jnp.zeros((own, LANES), jnp.float32)
    at = 0
    for low, high in cuts:
        for slot in range(pack.members):
            outs[at][...] = buf[slot, :, low:high]
            at += 1


def packed(pack, cuts, me, cells):
    own = cells.shape[2]
    outs = pl.pallas_call(
        functools.partial(pack_body, pack, cuts),
        out_shape=[
            jax.ShapeDtypeStruct((own, high - low), jnp.float32)
            for low, high in cuts
            for _ in range(pack.members)
        ],
        in_specs=[SMEM, VMEM],
        out_specs=[VMEM] * (len(cuts) * pack.members),
        scratch_shapes=[pltpu.VMEM((pack.members, own, pack.lanes), jnp.float32)],
        compiler_params=params(),
        name="pack",
    )(me, cells)
    return [outs[i * pack.members : (i + 1) * pack.members] for i in range(len(cuts))]


def unpack_body(pack, cuts, me_ref, *refs):
    parts, out_ref, buf = refs[:-2], refs[-2], refs[-1]
    me = me_ref[0]
    at = 0
    for low, high in cuts:
        for shift in range(pack.members):
            chunk = lax.rem(me - shift + pack.members, pack.members)
            buf[chunk, :, low:high] = parts[at][...]
            at += 1
    for row in range(pack.rows):
        x, z = divmod(row, pack.depth)
        for chunk, there, here, count in pack.runs(row):
            out_ref[x, z, :, here : here + count] = buf[chunk, :, there : there + count]
    start = pack.full * LANES
    for index in range(pack.tail_tiles):
        chunk, place = pack.tail_place(index)
        tile = buf[chunk, :, place : place + LANES]
        for k, row in enumerate(range(index * pack.group, min(pack.rows, (index + 1) * pack.group))):
            x, z = divmod(row, pack.depth)
            out_ref[x, z, :, start : start + pack.tail] = tile[:, k * pack.tail : (k + 1) * pack.tail]


def unpacked(pack, cuts, me, parts):
    own = parts[0].shape[0]
    return pl.pallas_call(
        functools.partial(unpack_body, pack, cuts),
        out_shape=jax.ShapeDtypeStruct((pack.width, pack.depth, own, pack.across), jnp.float32),
        in_specs=[SMEM] + [VMEM] * len(parts),
        out_specs=VMEM,
        scratch_shapes=[pltpu.VMEM((pack.members, own, pack.lanes), jnp.float32)],
        compiler_params=params(),
        name="unpack",
    )(me, *parts)


def distance_body(members, me_ref, *refs):
    parts, out_ref, all_ref = refs[:members], refs[members], refs[members + 1]
    own = parts[0].shape[0]
    me = me_ref[0]
    for shift in range(members):
        row = pl.multiple_of(lax.rem(me - shift + members, members) * own, own)
        all_ref[pl.ds(row, own), :] = parts[shift][...]
    cells = all_ref[...]
    cells = cells - cells[0:1, :]
    gram = lax.dot_general(
        cells,
        cells,
        (((1,), (1,)), ((), ())),
        precision=lax.Precision.HIGHEST,
        preferred_element_type=jnp.float32,
    )
    count = gram.shape[0]
    rows = lax.broadcasted_iota(jnp.int32, (count, count), 0)
    cols = lax.broadcasted_iota(jnp.int32, (count, count), 1)
    diag = jnp.where(rows == cols, gram, 0.0)
    down = jnp.sum(diag, axis=1, keepdims=True)
    along = jnp.sum(diag, axis=0, keepdims=True)
    out_ref[...] = jnp.where(rows == cols, 0.0, down + along - 2.0 * gram)


def distances(members, me, parts):
    own, lanes = parts[0].shape
    count = own * members
    return pl.pallas_call(
        functools.partial(distance_body, members),
        out_shape=jax.ShapeDtypeStruct((count, count), jnp.float32),
        in_specs=[SMEM] + [VMEM] * members,
        out_specs=VMEM,
        scratch_shapes=[pltpu.VMEM((count, lanes), jnp.float32)],
        compiler_params=params(),
        name="distances",
    )(me, *parts)


def update_body(members, low, me_ref, dist_ref, *refs):
    cells, grads = refs[:members], refs[members : 2 * members]
    outs = refs[2 * members : 3 * members]
    cell_ref, grad_ref, out_ref = refs[3 * members :]
    own, lanes = grads[0].shape
    count = own * members
    me = me_ref[0]
    for shift in range(members):
        row = pl.multiple_of(lax.rem(me - shift + members, members) * own, own)
        cell_ref[pl.ds(row, own), :] = cells[shift][:, low : low + lanes]
        grad_ref[pl.ds(row, own), :] = grads[shift][...]
    dist = dist_ref[...]
    band = jnp.sum(jnp.sum(dist, axis=1, keepdims=True), axis=0, keepdims=True) / (
        count * (count - 1) * math.log(count + 1)
    )
    kern = jnp.exp(-dist / band)
    total = jnp.sum(kern, axis=1, keepdims=True)
    cell = cell_ref[...]
    mixed = 0.5 * band * grad_ref[...] - cell
    pulled = jnp.dot(
        kern, mixed, precision=lax.Precision.HIGHEST, preferred_element_type=jnp.float32
    )
    out_ref[...] = cell + step_size * (pulled + total * cell)
    for shift in range(members):
        row = pl.multiple_of(lax.rem(me + shift, members) * own, own)
        outs[shift][...] = out_ref[pl.ds(row, own), :]


def updated(members, low, me, dist, cells, grads):
    own, lanes = grads[0].shape
    count = own * members
    return pl.pallas_call(
        functools.partial(update_body, members, low),
        out_shape=[jax.ShapeDtypeStruct((own, lanes), jnp.float32)] * members,
        in_specs=[SMEM, VMEM] + [VMEM] * (2 * members),
        out_specs=[VMEM] * members,
        scratch_shapes=[pltpu.VMEM((count, lanes), jnp.float32)] * 3,
        compiler_params=params(),
        name="update",
    )(me, dist, *cells, *grads)


def exchange(parts, members):
    return [parts[0]] + [
        lax.ppermute(parts[shift], "member", [(i, (i + shift) % members) for i in range(members)])
        for shift in range(1, members)
    ]


def medium_body(across, cells_ref, ghosts_ref, coef_ref, still_ref):
    width, depth, own, _ = cells_ref.shape
    lanes = coef_ref.shape[-1]
    start = (across // LANES) * LANES
    if lanes > start:
        edge = jnp.zeros((own, lanes - start), jnp.float32)

    def one(x, carry):
        for z in range(depth):
            if lanes > start:
                coef_ref[x, z, :, start:] = edge
                still_ref[x, z, :, start:] = edge
            speed = courant * (1.0 + 0.3 * jnp.tanh(cells_ref[x, z]))
            coef_ref[x, z, :, :across] = speed * speed
            total = None
            for offset in range(1, GHOST + 1):
                terms = []
                if z - offset < 0:
                    terms.append(ghosts_ref[x, GHOST + z - offset])
                if z + offset >= depth:
                    terms.append(ghosts_ref[x, GHOST + z + offset - depth])
                for term in terms:
                    part = weights[offset] * term
                    total = part if total is None else total + part
            if total is None:
                total = jnp.zeros((own, across), jnp.float32)
            still_ref[x, z, :, :across] = total
        return carry

    lax.fori_loop(0, width, one, 0)


def medium(across, lanes, cells, ghosts):
    shape = jax.ShapeDtypeStruct(cells.shape[:3] + (lanes,), jnp.float32)
    return pl.pallas_call(
        functools.partial(medium_body, across),
        out_shape=[shape, shape],
        in_specs=[VMEM, VMEM],
        out_specs=[VMEM, VMEM],
        compiler_params=params(),
        name="medium",
    )(cells, ghosts)


def wave_body(amplitude, last, source_ref, left_ref, right_ref, now_ref, prev_ref, coef_ref, still_ref, *refs):
    out_ref, wide = refs[0], refs[-1]
    width, depth, own, lanes = now_ref.shape
    wide[0:GHOST] = left_ref[...]
    wide[GHOST : GHOST + width] = now_ref[...]
    wide[GHOST + width :] = right_ref[...]

    def one(x, carry):
        for z in range(depth):
            center = wide[x + GHOST, z]
            total = 3.0 * weights[0] * center + still_ref[x, z]
            for offset in range(1, GHOST + 1):
                pair = wide[x + GHOST + offset, z] + wide[x + GHOST - offset, z]
                pair = pair + pltpu.roll(center, offset, 1) + pltpu.roll(center, lanes - offset, 1)
                if z - offset >= 0:
                    pair = pair + wide[x + GHOST, z - offset]
                if z + offset < depth:
                    pair = pair + wide[x + GHOST, z + offset]
                total = total + weights[offset] * pair
            out_ref[x, z] = 2.0 * center - prev_ref[x, z] + coef_ref[x, z] * total
        return carry

    lax.fori_loop(0, width, one, 0)
    rows = lax.broadcasted_iota(jnp.int32, (own, lanes), 0)
    cols = lax.broadcasted_iota(jnp.int32, (own, lanes), 1)
    for index in range(own):
        x, y = source_ref[0, index], source_ref[1, index]

        @pl.when((x >= 0) & (x < width))
        def _(x=x, y=y, index=index):
            spot = (rows == index) & (cols == y)
            out_ref[x, 0] = out_ref[x, 0] + jnp.where(spot, amplitude, 0.0)

    if not last:
        head_ref, tail_ref = refs[1], refs[2]
        head_ref[...] = out_ref[0:GHOST]
        tail_ref[...] = out_ref[width - GHOST :]


def wave_step(amplitude, last, source, left, right, now, prev, coef, still):
    width, depth, own, lanes = now.shape
    out = jax.ShapeDtypeStruct(now.shape, jnp.float32)
    edge = jax.ShapeDtypeStruct((GHOST,) + now.shape[1:], jnp.float32)
    outs = [out] if last else [out, edge, edge]
    return pl.pallas_call(
        functools.partial(wave_body, amplitude, last),
        out_shape=outs,
        in_specs=[SMEM] + [VMEM] * 6,
        out_specs=[VMEM] * len(outs),
        scratch_shapes=[pltpu.VMEM((width + 2 * GHOST, depth, own, lanes), jnp.float32)],
        compiler_params=params(),
        name="wave",
    )(source, left, right, now, prev, coef, still)


def shards(cuts_of, particles, loglik_grad, wave_prev, wave_now, ghosts, src_cell):
    own, depth, width, across = particles.shape
    members = lax.axis_size("member")
    spaces = lax.axis_size("space")
    member_idx = lax.axis_index("member")
    space_idx = lax.axis_index("space")
    pack = Packing(width, depth, across, members)
    whole = [(0, pack.lanes)]
    cuts = cuts_of(pack)
    me = jnp.reshape(member_idx, (1,)).astype(jnp.int32)
    lanes = -(-(across + GHOST) // LANES) * LANES

    def turned(array):
        return jnp.transpose(array, (2, 1, 0, 3))

    cells = turned(particles)
    cell_parts = exchange(packed(pack, whole, me, cells)[0], members)
    grad_parts = [exchange(part, members) for part in packed(pack, cuts, me, turned(loglik_grad))]

    dist = distances(members, me, cell_parts)
    dist = jnp.sum(lax.all_gather(dist, "space", axis=0), axis=0)
    dist = sum(exchange([dist] * members, members))

    moved = []
    for (low, _), grads in zip(cuts, grad_parts):
        moved += exchange(updated(members, low, me, dist, cell_parts, grads), members)
    new_particles = turned(unpacked(pack, cuts, me, moved))

    def wide(array):
        return jnp.pad(turned(array), ((0, 0), (0, 0), (0, 0), (0, lanes - across)))

    source = jnp.stack([src_cell // across - space_idx * width, src_cell % across])
    coef, still = medium(across, lanes, cells, turned(ghosts))
    prev, now = wide(wave_prev), wide(wave_now)
    head, tail = now[:GHOST], now[width - GHOST :]
    for step in range(STEPS):
        left = lax.ppermute(tail, "space", [(i, i + 1) for i in range(spaces - 1)])
        right = lax.ppermute(head, "space", [(i + 1, i) for i in range(spaces - 1)])
        amplitude = 2.0 * math.cos(1.3 * step)
        last = step == STEPS - 1
        outs = wave_step(amplitude, last, source, left, right, now, prev, coef, still)
        if not last:
            head, tail = outs[1], outs[2]
        prev, now = now, outs[0]
    return new_particles, turned(prev[..., :across]), turned(now[..., :across])


def one_cut(pack):
    return [(0, pack.lanes)]


def solution(mesh):
    spec = P("member", None, "space", None)
    return jax.shard_map(
        functools.partial(shards, one_cut),
        mesh=mesh,
        in_specs=(spec, spec, spec, spec, spec, P("member")),
        out_specs=(spec, spec, spec),
        check_vma=False,
    )
```

```python
import functools
import math

import jax
import jax.numpy as jnp
from jax import lax
from jax.experimental import pallas as pl
from jax.experimental.pallas import tpu as pltpu
from jax.sharding import PartitionSpec as P

GHOST = 4
STEPS = 4
LANES = 128

weights = (-205.0 / 72.0, 8.0 / 5.0, -1.0 / 5.0, 8.0 / 315.0, -1.0 / 560.0)
step_size = 0.25
courant = 0.3

VMEM = pl.BlockSpec(memory_space=pltpu.VMEM)
SMEM = pl.BlockSpec(memory_space=pltpu.SMEM)


ANY = pl.BlockSpec(memory_space=pl.ANY)


def call(body, name, out_shape, in_specs, out_specs, operands, scratch_shapes=(), after=()):
    count = len(operands)

    def ordered(*refs):
        body(*refs[:count], *refs[count + len(after) :])

    return pl.pallas_call(
        ordered,
        out_shape=out_shape,
        in_specs=in_specs + [ANY] * len(after),
        out_specs=out_specs,
        scratch_shapes=scratch_shapes,
        compiler_params=pltpu.CompilerParams(vmem_limit_bytes=40 << 20),
        name=name,
    )(*operands, *after)


class Packing:
    def __init__(self, width, depth, across, members):
        self.width, self.depth, self.across, self.members = width, depth, across, members
        self.rows = width * depth
        self.full = across // LANES
        self.tail = across % LANES
        self.group = LANES // self.tail if self.tail else 1
        self.tail_tiles = -(-self.rows // self.group) if self.tail else 0
        total = self.rows * self.full + self.tail_tiles
        self.tiles = -(-total // members)
        self.lanes = self.tiles * LANES
        self.spare = self.tiles * members - total

    def runs(self, row):
        tile, at, left = row * self.full, 0, self.full
        while left:
            chunk, place = divmod(tile, self.tiles)
            count = min(left, self.tiles - place)
            yield chunk, place * LANES, at * LANES, count * LANES
            tile, at, left = tile + count, at + count, left - count

    def tail_place(self, index):
        chunk, place = divmod(self.rows * self.full + index, self.tiles)
        return chunk, place * LANES


def pack_body(pack, cuts, me_ref, cells_ref, *refs):
    outs, buf = refs[:-1], refs[-1]
    own = cells_ref.shape[2]
    me = me_ref[0]
    slots = [lax.rem(chunk - me + pack.members, pack.members) for chunk in range(pack.members)]
    for row in range(pack.rows):
        x, z = divmod(row, pack.depth)
        for chunk, there, here, count in pack.runs(row):
            buf[slots[chunk], :, there : there + count] = cells_ref[x, z, :, here : here + count]
    start = pack.full * LANES
    for index in range(pack.tail_tiles):
        chunk, place = pack.tail_place(index)
        pieces = []
        for row in range(index * pack.group, min(pack.rows, (index + 1) * pack.group)):
            x, z = divmod(row, pack.depth)
            pieces.append(cells_ref[x, z, :, start : start + pack.tail])
        empty = LANES - pack.tail * len(pieces)
        if empty:
            pieces.append(jnp.zeros((own, empty), jnp.float32))
        buf[slots[chunk], :, place : place + LANES] = jnp.concatenate(pieces, axis=1)
    for index in range(pack.spare):
        chunk, place = pack.tail_place(pack.tail_tiles + index)
        buf[slots[chunk], :, place : place + LANES] = jnp.zeros((own, LANES), jnp.float32)
    at = 0
    for low, high in cuts:
        for slot in range(pack.members):
            outs[at][...] = buf[slot, :, low:high]
            at += 1


def packed(pack, cuts, me, cells, after=()):
    own = cells.shape[2]
    outs = call(
        functools.partial(pack_body, pack, cuts),
        "pack",
        out_shape=[
            jax.ShapeDtypeStruct((own, high - low), jnp.float32)
            for low, high in cuts
            for _ in range(pack.members)
        ],
        in_specs=[SMEM, VMEM],
        out_specs=[VMEM] * (len(cuts) * pack.members),
        operands=[me, cells],
        scratch_shapes=[pltpu.VMEM((pack.members, own, pack.lanes), jnp.float32)],
        after=after,
    )
    return [outs[i * pack.members : (i + 1) * pack.members] for i in range(len(cuts))]


def unpack_body(pack, cuts, me_ref, *refs):
    parts, out_ref, buf = refs[:-2], refs[-2], refs[-1]
    me = me_ref[0]
    at = 0
    for low, high in cuts:
        for shift in range(pack.members):
            chunk = lax.rem(me - shift + pack.members, pack.members)
            buf[chunk, :, low:high] = parts[at][...]
            at += 1
    for row in range(pack.rows):
        x, z = divmod(row, pack.depth)
        for chunk, there, here, count in pack.runs(row):
            out_ref[x, z, :, here : here + count] = buf[chunk, :, there : there + count]
    start = pack.full * LANES
    for index in range(pack.tail_tiles):
        chunk, place = pack.tail_place(index)
        tile = buf[chunk, :, place : place + LANES]
        for k, row in enumerate(range(index * pack.group, min(pack.rows, (index + 1) * pack.group))):
            x, z = divmod(row, pack.depth)
            out_ref[x, z, :, start : start + pack.tail] = tile[:, k * pack.tail : (k + 1) * pack.tail]


def unpacked(pack, cuts, me, parts, after=()):
    own = parts[0].shape[0]
    return call(
        functools.partial(unpack_body, pack, cuts),
        "unpack",
        out_shape=jax.ShapeDtypeStruct((pack.width, pack.depth, own, pack.across), jnp.float32),
        in_specs=[SMEM] + [VMEM] * len(parts),
        out_specs=VMEM,
        operands=[me, *parts],
        scratch_shapes=[pltpu.VMEM((pack.members, own, pack.lanes), jnp.float32)],
        after=after,
    )


def distance_body(members, me_ref, *refs):
    parts, out_ref, all_ref = refs[:members], refs[members], refs[members + 1]
    own = parts[0].shape[0]
    me = me_ref[0]
    for shift in range(members):
        row = pl.multiple_of(lax.rem(me - shift + members, members) * own, own)
        all_ref[pl.ds(row, own), :] = parts[shift][...]
    cells = all_ref[...]
    cells = cells - cells[0:1, :]
    gram = lax.dot_general(
        cells,
        cells,
        (((1,), (1,)), ((), ())),
        precision=lax.Precision.HIGHEST,
        preferred_element_type=jnp.float32,
    )
    count = gram.shape[0]
    rows = lax.broadcasted_iota(jnp.int32, (count, count), 0)
    cols = lax.broadcasted_iota(jnp.int32, (count, count), 1)
    diag = jnp.where(rows == cols, gram, 0.0)
    down = jnp.sum(diag, axis=1, keepdims=True)
    along = jnp.sum(diag, axis=0, keepdims=True)
    out_ref[...] = jnp.where(rows == cols, 0.0, down + along - 2.0 * gram)


def distances(members, me, parts, after=()):
    own, lanes = parts[0].shape
    count = own * members
    return call(
        functools.partial(distance_body, members),
        "distances",
        out_shape=jax.ShapeDtypeStruct((count, count), jnp.float32),
        in_specs=[SMEM] + [VMEM] * members,
        out_specs=VMEM,
        operands=[me, *parts],
        scratch_shapes=[pltpu.VMEM((count, lanes), jnp.float32)],
        after=after,
    )


def update_body(members, low, me_ref, dist_ref, *refs):
    cells, grads = refs[:members], refs[members : 2 * members]
    outs = refs[2 * members : 3 * members]
    cell_ref, grad_ref, out_ref = refs[3 * members :]
    own, lanes = grads[0].shape
    count = own * members
    me = me_ref[0]
    for shift in range(members):
        row = pl.multiple_of(lax.rem(me - shift + members, members) * own, own)
        cell_ref[pl.ds(row, own), :] = cells[shift][:, low : low + lanes]
        grad_ref[pl.ds(row, own), :] = grads[shift][...]
    dist = dist_ref[...]
    band = jnp.sum(jnp.sum(dist, axis=1, keepdims=True), axis=0, keepdims=True) / (
        count * (count - 1) * math.log(count + 1)
    )
    kern = jnp.exp(-dist / band)
    total = jnp.sum(kern, axis=1, keepdims=True)
    cell = cell_ref[...]
    mixed = 0.5 * band * grad_ref[...] - cell
    pulled = jnp.dot(
        kern, mixed, precision=lax.Precision.HIGHEST, preferred_element_type=jnp.float32
    )
    out_ref[...] = cell + step_size * (pulled + total * cell)
    for shift in range(members):
        row = pl.multiple_of(lax.rem(me + shift, members) * own, own)
        outs[shift][...] = out_ref[pl.ds(row, own), :]


def updated(members, low, me, dist, cells, grads, after=()):
    own, lanes = grads[0].shape
    count = own * members
    return call(
        functools.partial(update_body, members, low),
        "update",
        out_shape=[jax.ShapeDtypeStruct((own, lanes), jnp.float32)] * members,
        in_specs=[SMEM, VMEM] + [VMEM] * (2 * members),
        out_specs=[VMEM] * members,
        operands=[me, dist, *cells, *grads],
        scratch_shapes=[pltpu.VMEM((count, lanes), jnp.float32)] * 3,
        after=after,
    )


def exchange(parts, members):
    return [parts[0]] + [
        lax.ppermute(parts[shift], "member", [(i, (i + shift) % members) for i in range(members)])
        for shift in range(1, members)
    ]


def medium_body(across, cells_ref, ghosts_ref, coef_ref, still_ref):
    width, depth, own, _ = cells_ref.shape
    lanes = coef_ref.shape[-1]
    start = (across // LANES) * LANES
    if lanes > start:
        edge = jnp.zeros((own, lanes - start), jnp.float32)

    def one(x, carry):
        for z in range(depth):
            if lanes > start:
                coef_ref[x, z, :, start:] = edge
                still_ref[x, z, :, start:] = edge
            speed = courant * (1.0 + 0.3 * jnp.tanh(cells_ref[x, z]))
            coef_ref[x, z, :, :across] = speed * speed
            total = None
            for offset in range(1, GHOST + 1):
                terms = []
                if z - offset < 0:
                    terms.append(ghosts_ref[x, GHOST + z - offset])
                if z + offset >= depth:
                    terms.append(ghosts_ref[x, GHOST + z + offset - depth])
                for term in terms:
                    part = weights[offset] * term
                    total = part if total is None else total + part
            if total is None:
                total = jnp.zeros((own, across), jnp.float32)
            still_ref[x, z, :, :across] = total
        return carry

    lax.fori_loop(0, width, one, 0)


def medium(across, lanes, cells, ghosts, after=()):
    shape = jax.ShapeDtypeStruct(cells.shape[:3] + (lanes,), jnp.float32)
    return call(
        functools.partial(medium_body, across),
        "medium",
        out_shape=[shape, shape],
        in_specs=[VMEM, VMEM],
        out_specs=[VMEM, VMEM],
        operands=[cells, ghosts],
        after=after,
    )


def wave_body(amplitude, last, source_ref, left_ref, right_ref, now_ref, prev_ref, coef_ref, still_ref, *refs):
    out_ref, wide = refs[0], refs[-1]
    width, depth, own, lanes = now_ref.shape
    wide[0:GHOST] = left_ref[...]
    wide[GHOST : GHOST + width] = now_ref[...]
    wide[GHOST + width :] = right_ref[...]

    def one(x, carry):
        for z in range(depth):
            center = wide[x + GHOST, z]
            total = 3.0 * weights[0] * center + still_ref[x, z]
            for offset in range(1, GHOST + 1):
                pair = wide[x + GHOST + offset, z] + wide[x + GHOST - offset, z]
                pair = pair + pltpu.roll(center, offset, 1) + pltpu.roll(center, lanes - offset, 1)
                if z - offset >= 0:
                    pair = pair + wide[x + GHOST, z - offset]
                if z + offset < depth:
                    pair = pair + wide[x + GHOST, z + offset]
                total = total + weights[offset] * pair
            out_ref[x, z] = 2.0 * center - prev_ref[x, z] + coef_ref[x, z] * total
        return carry

    lax.fori_loop(0, width, one, 0)
    rows = lax.broadcasted_iota(jnp.int32, (own, lanes), 0)
    cols = lax.broadcasted_iota(jnp.int32, (own, lanes), 1)
    for index in range(own):
        x, y = source_ref[0, index], source_ref[1, index]

        @pl.when((x >= 0) & (x < width))
        def _(x=x, y=y, index=index):
            spot = (rows == index) & (cols == y)
            out_ref[x, 0] = out_ref[x, 0] + jnp.where(spot, amplitude, 0.0)

    if not last:
        head_ref, tail_ref = refs[1], refs[2]
        head_ref[...] = out_ref[0:GHOST]
        tail_ref[...] = out_ref[width - GHOST :]


def wave_step(amplitude, last, source, left, right, now, prev, coef, still, after=()):
    width, depth, own, lanes = now.shape
    out = jax.ShapeDtypeStruct(now.shape, jnp.float32)
    edge = jax.ShapeDtypeStruct((GHOST,) + now.shape[1:], jnp.float32)
    outs = [out] if last else [out, edge, edge]
    return call(
        functools.partial(wave_body, amplitude, last),
        "wave",
        out_shape=outs,
        in_specs=[SMEM] + [VMEM] * 6,
        out_specs=[VMEM] * len(outs),
        operands=[source, left, right, now, prev, coef, still],
        scratch_shapes=[pltpu.VMEM((width + 2 * GHOST, depth, own, lanes), jnp.float32)],
        after=after,
    )


def shards(cuts_of, particles, loglik_grad, wave_prev, wave_now, ghosts, src_cell):
    own, depth, width, across = particles.shape
    members = lax.axis_size("member")
    spaces = lax.axis_size("space")
    member_idx = lax.axis_index("member")
    space_idx = lax.axis_index("space")
    pack = Packing(width, depth, across, members)
    whole = [(0, pack.lanes)]
    cuts = cuts_of(pack)
    me = jnp.reshape(member_idx, (1,)).astype(jnp.int32)
    lanes = -(-(across + GHOST) // LANES) * LANES

    def turned(array):
        return jnp.transpose(array, (2, 1, 0, 3))

    def wide(array):
        return jnp.pad(turned(array), ((0, 0), (0, 0), (0, 0), (0, lanes - across)))

    cells = turned(particles)
    cell_parts = exchange(packed(pack, whole, me, cells)[0], members)
    grad_parts = [exchange(part, members) for part in packed(pack, cuts, me, turned(loglik_grad))]

    source = jnp.stack([src_cell // across - space_idx * width, src_cell % across])
    coef, still = medium(across, lanes, cells, turned(ghosts))
    waves = [wide(wave_prev), wide(wave_now)]
    head, tail = waves[1][:GHOST], waves[1][width - GHOST :]
    for step in range(STEPS):
        left = lax.ppermute(tail, "space", [(i, i + 1) for i in range(spaces - 1)])
        right = lax.ppermute(head, "space", [(i + 1, i) for i in range(spaces - 1)])
        amplitude = 2.0 * math.cos(1.3 * step)
        last = step == STEPS - 1
        outs = wave_step(amplitude, last, source, left, right, waves[-1], waves[-2], coef, still)
        if not last:
            head, tail = outs[1], outs[2]
        waves.append(outs[0])

    early = waves[2 + STEPS // 2 - 1]
    dist = distances(members, me, cell_parts, after=[early])
    dist = jnp.sum(lax.all_gather(dist, "space", axis=0), axis=0)
    dist = sum(exchange([dist] * members, members))

    moved = []
    for (low, _), grads in zip(cuts, grad_parts):
        moved += exchange(updated(members, low, me, dist, cell_parts, grads), members)
    new_particles = turned(unpacked(pack, cuts, me, moved, after=[waves[-1]]))
    return new_particles, turned(waves[-2][..., :across]), turned(waves[-1][..., :across])


def one_cut(pack):
    return [(0, pack.lanes)]


def solution(mesh):
    spec = P("member", None, "space", None)
    return jax.shard_map(
        functools.partial(shards, one_cut),
        mesh=mesh,
        in_specs=(spec, spec, spec, spec, spec, P("member")),
        out_specs=(spec, spec, spec),
        check_vma=False,
    )
```

```python
import functools
import math

import jax
import jax.numpy as jnp
from jax import lax
from jax.experimental import pallas as pl
from jax.experimental.pallas import tpu as pltpu
from jax.sharding import PartitionSpec as P


GHOST = 4
STEPS = 4
LANES = 128

weights = (-205.0 / 72.0, 8.0 / 5.0, -1.0 / 5.0, 8.0 / 315.0, -1.0 / 560.0)
step_size = 0.25
courant = 0.3

VMEM = pl.BlockSpec(memory_space=pltpu.VMEM)
SMEM = pl.BlockSpec(memory_space=pltpu.SMEM)


ANY = pl.BlockSpec(memory_space=pl.ANY)


def held(shape, space=pltpu.VMEM):
    return space(tuple(shape), jnp.float32)


def call(body, out_shape, in_specs, out_specs, operands, scratch_shapes=(), after=()):
    count = len(operands)

    def ordered(*refs):
        body(*refs[:count], *refs[count + len(after) :])

    return pl.pallas_call(
        ordered,
        out_shape=out_shape,
        in_specs=in_specs + [ANY] * len(after),
        out_specs=out_specs,
        scratch_shapes=scratch_shapes,
        compiler_params=pltpu.CompilerParams(vmem_limit_bytes=24 << 20),
    )(*operands, *after)


class Packing:
    def __init__(self, width, depth, across, members):
        self.width, self.depth, self.across, self.members = width, depth, across, members
        self.rows = width * depth
        self.full = across // LANES
        self.tail = across % LANES
        self.group = LANES // self.tail if self.tail else 1
        self.tail_tiles = -(-self.rows // self.group) if self.tail else 0
        total = self.rows * self.full + self.tail_tiles
        self.tiles = -(-total // members)
        self.lanes = self.tiles * LANES
        self.spare = self.tiles * members - total

    def runs(self, row):
        tile, at, left = row * self.full, 0, self.full
        while left:
            chunk, place = divmod(tile, self.tiles)
            count = min(left, self.tiles - place)
            yield chunk, place * LANES, at * LANES, count * LANES
            tile, at, left = tile + count, at + count, left - count

    def tail_place(self, index):
        chunk, place = divmod(self.rows * self.full + index, self.tiles)
        return chunk, place * LANES


def pack_body(pack, cuts, me_ref, cells_ref, *refs):
    outs, buf = refs[:-1], refs[-1]
    own = cells_ref.shape[2]
    me = me_ref[0]
    slots = [lax.rem(chunk - me + pack.members, pack.members) for chunk in range(pack.members)]
    for row in range(pack.rows):
        x, z = divmod(row, pack.depth)
        for chunk, there, here, count in pack.runs(row):
            buf[slots[chunk], :, there : there + count] = cells_ref[x, z, :, here : here + count]
    start = pack.full * LANES
    for index in range(pack.tail_tiles):
        chunk, place = pack.tail_place(index)
        pieces = []
        for row in range(index * pack.group, min(pack.rows, (index + 1) * pack.group)):
            x, z = divmod(row, pack.depth)
            pieces.append(cells_ref[x, z, :, start : start + pack.tail])
        empty = LANES - pack.tail * len(pieces)
        if empty:
            pieces.append(jnp.zeros((own, empty), jnp.float32))
        buf[slots[chunk], :, place : place + LANES] = jnp.concatenate(pieces, axis=1)
    for index in range(pack.spare):
        chunk, place = pack.tail_place(pack.tail_tiles + index)
        buf[slots[chunk], :, place : place + LANES] = jnp.zeros((own, LANES), jnp.float32)
    at = 0
    for low, high in cuts:
        for slot in range(pack.members):
            outs[at][...] = buf[slot, :, low:high]
            at += 1


def packed(pack, cuts, me, cells, after=()):
    own = cells.shape[2]
    outs = call(
        functools.partial(pack_body, pack, cuts),
        out_shape=[
            held((own, high - low), pltpu.HBM)
            for low, high in cuts
            for _ in range(pack.members)
        ],
        in_specs=[SMEM, VMEM],
        out_specs=[VMEM] * (len(cuts) * pack.members),
        operands=[me, cells],
        scratch_shapes=[pltpu.VMEM((pack.members, own, pack.lanes), jnp.float32)],
        after=after,
    )
    return [outs[i * pack.members : (i + 1) * pack.members] for i in range(len(cuts))]


def unpack_body(pack, cuts, me_ref, *refs):
    parts, out_ref, buf = refs[:-2], refs[-2], refs[-1]
    me = me_ref[0]
    at = 0
    for low, high in cuts:
        for shift in range(pack.members):
            chunk = lax.rem(me - shift + pack.members, pack.members)
            buf[chunk, :, low:high] = parts[at][...]
            at += 1
    for row in range(pack.rows):
        x, z = divmod(row, pack.depth)
        for chunk, there, here, count in pack.runs(row):
            out_ref[x, z, :, here : here + count] = buf[chunk, :, there : there + count]
    start = pack.full * LANES
    for index in range(pack.tail_tiles):
        chunk, place = pack.tail_place(index)
        tile = buf[chunk, :, place : place + LANES]
        for k, row in enumerate(range(index * pack.group, min(pack.rows, (index + 1) * pack.group))):
            x, z = divmod(row, pack.depth)
            out_ref[x, z, :, start : start + pack.tail] = tile[:, k * pack.tail : (k + 1) * pack.tail]


def unpacked(pack, cuts, me, parts, after=()):
    own = parts[0].shape[0]
    return call(
        functools.partial(unpack_body, pack, cuts),
        out_shape=[jax.ShapeDtypeStruct((pack.width, pack.depth, own, pack.across), jnp.float32)],
        in_specs=[SMEM] + [VMEM] * len(parts),
        out_specs=[VMEM],
        operands=[me, *parts],
        scratch_shapes=[pltpu.VMEM((pack.members, own, pack.lanes), jnp.float32)],
        after=after,
    )


def distance_body(members, me_ref, *refs):
    parts, out_ref, all_ref = refs[:members], refs[members], refs[members + 1]
    own = parts[0].shape[0]
    me = me_ref[0]
    for shift in range(members):
        row = pl.multiple_of(lax.rem(me - shift + members, members) * own, own)
        all_ref[pl.ds(row, own), :] = parts[shift][...]
    cells = all_ref[...]
    cells = cells - cells[0:1, :]
    gram = lax.dot_general(
        cells,
        cells,
        (((1,), (1,)), ((), ())),
        precision=lax.Precision.HIGHEST,
        preferred_element_type=jnp.float32,
    )
    count = gram.shape[0]
    rows = lax.broadcasted_iota(jnp.int32, (count, count), 0)
    cols = lax.broadcasted_iota(jnp.int32, (count, count), 1)
    diag = jnp.where(rows == cols, gram, 0.0)
    down = jnp.sum(diag, axis=1, keepdims=True)
    along = jnp.sum(diag, axis=0, keepdims=True)
    dist = jnp.where(rows == cols, 0.0, down + along - 2.0 * gram)
    for member in range(members):
        out_ref[:, member * count : (member + 1) * count] = dist[member * own : (member + 1) * own]


def distances(members, me, parts, after=()):
    own, lanes = parts[0].shape
    count = own * members
    return call(
        functools.partial(distance_body, members),
        out_shape=[held((own, members * count))],
        in_specs=[SMEM] + [VMEM] * members,
        out_specs=[VMEM],
        operands=[me, *parts],
        scratch_shapes=[pltpu.VMEM((count, lanes), jnp.float32)],
        after=after,
    )


def update_body(members, low, me_ref, dist_ref, *refs):
    cells, grads = refs[:members], refs[members : 2 * members]
    outs = refs[2 * members : 3 * members]
    cell_ref, grad_ref, out_ref = refs[3 * members :]
    own, lanes = grads[0].shape
    count = own * members
    me = me_ref[0]
    for shift in range(members):
        row = pl.multiple_of(lax.rem(me - shift + members, members) * own, own)
        cell_ref[pl.ds(row, own), :] = cells[shift][:, low : low + lanes]
        grad_ref[pl.ds(row, own), :] = grads[shift][...]
    dist = jnp.concatenate(
        [dist_ref[:, member * count : (member + 1) * count] for member in range(members)], axis=0
    )
    band = jnp.sum(jnp.sum(dist, axis=1, keepdims=True), axis=0, keepdims=True) / (
        count * (count - 1) * math.log(count + 1)
    )
    kern = jnp.exp(-dist / band)
    total = jnp.sum(kern, axis=1, keepdims=True)
    cell = cell_ref[...]
    mixed = 0.5 * band * grad_ref[...] - cell
    pulled = jnp.dot(
        kern, mixed, precision=lax.Precision.HIGHEST, preferred_element_type=jnp.float32
    )
    out_ref[...] = cell + step_size * (pulled + total * cell)
    for shift in range(members):
        row = pl.multiple_of(lax.rem(me + shift, members) * own, own)
        outs[shift][...] = out_ref[pl.ds(row, own), :]


def updated(members, low, me, dist, cells, grads, after=()):
    own, lanes = grads[0].shape
    count = own * members
    return call(
        functools.partial(update_body, members, low),
        out_shape=[held((own, lanes), pltpu.HBM)] * members,
        in_specs=[SMEM, VMEM] + [VMEM] * (2 * members),
        out_specs=[VMEM] * members,
        operands=[me, dist, *cells, *grads],
        scratch_shapes=[pltpu.VMEM((count, lanes), jnp.float32)] * 3,
        after=after,
    )


def exchange(parts, members):
    return [parts[0]] + [
        lax.ppermute(parts[shift], "member", [(i, (i + shift) % members) for i in range(members)])
        for shift in range(1, members)
    ]


def spread_rows(across, cells_ref, out_ref):
    width, depth, own, lanes = out_ref.shape
    start = (across // LANES) * LANES
    if lanes > start:
        edge = jnp.zeros((own, lanes - start), jnp.float32)

    def one(x, carry):
        for z in range(depth):
            if lanes > start:
                out_ref[x, z, :, start:] = edge
            out_ref[x, z, :, :across] = cells_ref[x, z]
        return carry

    lax.fori_loop(0, width, one, 0)


def spread_body(across, now_ref, out_ref, head_ref, tail_ref):
    width = now_ref.shape[0]
    spread_rows(across, now_ref, out_ref)
    head_ref[...] = out_ref[0:GHOST]
    tail_ref[...] = out_ref[width - GHOST :]


def spread(across, lanes, now, after=()):
    out = held(now.shape[:3] + (lanes,))
    edge = held((GHOST,) + now.shape[1:3] + (lanes,))
    return call(
        functools.partial(spread_body, across),
        out_shape=[out, edge, edge],
        in_specs=[VMEM],
        out_specs=[VMEM] * 3,
        operands=[now],
        after=after,
    )


def medium_body(across, cells_ref, ghosts_ref, prev_ref, coef_ref, still_ref, wide_ref):
    width, depth, own, _ = cells_ref.shape
    lanes = coef_ref.shape[-1]
    start = (across // LANES) * LANES
    spread_rows(across, prev_ref, wide_ref)
    if lanes > start:
        edge = jnp.zeros((own, lanes - start), jnp.float32)

    def one(x, carry):
        for z in range(depth):
            if lanes > start:
                coef_ref[x, z, :, start:] = edge
                still_ref[x, z, :, start:] = edge
            speed = courant * (1.0 + 0.3 * jnp.tanh(cells_ref[x, z]))
            coef_ref[x, z, :, :across] = speed * speed
            total = None
            for offset in range(1, GHOST + 1):
                terms = []
                if z - offset < 0:
                    terms.append(ghosts_ref[x, GHOST + z - offset])
                if z + offset >= depth:
                    terms.append(ghosts_ref[x, GHOST + z + offset - depth])
                for term in terms:
                    part = weights[offset] * term
                    total = part if total is None else total + part
            if total is None:
                total = jnp.zeros((own, across), jnp.float32)
            still_ref[x, z, :, :across] = total
        return carry

    lax.fori_loop(0, width, one, 0)


def medium(across, lanes, cells, ghosts, prev, after=()):
    shape = held(cells.shape[:3] + (lanes,))
    return call(
        functools.partial(medium_body, across),
        out_shape=[shape] * 3,
        in_specs=[VMEM] * 3,
        out_specs=[VMEM] * 3,
        operands=[cells, ghosts, prev],
        after=after,
    )


def wave_body(amplitude, last, spot_ref, left_ref, right_ref, now_ref, prev_ref, coef_ref, still_ref, *refs):
    out_ref, wide = refs[0], refs[-1]
    width, depth, own, lanes = now_ref.shape
    wide[0:GHOST] = left_ref[...]
    wide[GHOST : GHOST + width] = now_ref[...]
    wide[GHOST + width :] = right_ref[...]
    cols = lax.broadcasted_iota(jnp.int32, (own, lanes), 1)
    spot = jnp.broadcast_to(spot_ref[:, 0:1], (own, lanes)) - cols

    def one(x, carry):
        for z in range(depth):
            center = wide[x + GHOST, z]
            total = 3.0 * weights[0] * center + still_ref[x, z]
            for offset in range(1, GHOST + 1):
                pair = wide[x + GHOST + offset, z] + wide[x + GHOST - offset, z]
                pair = pair + pltpu.roll(center, offset, 1) + pltpu.roll(center, lanes - offset, 1)
                if z - offset >= 0:
                    pair = pair + wide[x + GHOST, z - offset]
                if z + offset < depth:
                    pair = pair + wide[x + GHOST, z + offset]
                total = total + weights[offset] * pair
            value = 2.0 * center - prev_ref[x, z] + coef_ref[x, z] * total
            if z == 0:
                value = value + jnp.where(spot == x * lanes, amplitude, 0.0)
            out_ref[x, z] = value
        return carry

    lax.fori_loop(0, width, one, 0)
    if not last:
        head_ref, tail_ref = refs[1], refs[2]
        head_ref[...] = out_ref[0:GHOST]
        tail_ref[...] = out_ref[width - GHOST :]


def wave_step(amplitude, last, spot, left, right, now, prev, coef, still, after=()):
    width, depth, own, lanes = now.shape
    out = held(now.shape)
    edge = held((GHOST,) + now.shape[1:])
    outs = [out] if last else [out, edge, edge]
    return call(
        functools.partial(wave_body, amplitude, last),
        out_shape=outs,
        in_specs=[VMEM] * 7,
        out_specs=[VMEM] * len(outs),
        operands=[spot, left, right, now, prev, coef, still],
        scratch_shapes=[pltpu.VMEM((width + 2 * GHOST, depth, own, lanes), jnp.float32)],
        after=after,
    )


def shards(cuts_of, particles, loglik_grad, wave_prev, wave_now, ghosts, src_cell):
    own, depth, width, across = particles.shape
    members = lax.axis_size("member")
    spaces = lax.axis_size("space")
    member_idx = lax.axis_index("member")
    space_idx = lax.axis_index("space")
    pack = Packing(width, depth, across, members)
    whole = [(0, pack.lanes)]
    cuts = cuts_of(pack)
    me = jnp.reshape(member_idx, (1,)).astype(jnp.int32)
    lanes = -(-(across + GHOST) // LANES) * LANES

    def turned(array):
        return jnp.transpose(array, (2, 1, 0, 3))

    cells = turned(particles)
    ready = packed(pack, whole, me, cells)[0]
    ready, loglik_grad, wave_prev, wave_now, ghosts, src_cell = lax.optimization_barrier(
        (ready, loglik_grad, wave_prev, wave_now, ghosts, src_cell)
    )
    cell_parts = exchange(ready, members)

    now, head, tail = spread(across, lanes, turned(wave_now))
    spot = (src_cell // across - space_idx * width) * lanes + src_cell % across
    spot = jnp.broadcast_to(spot[:, None], (own, LANES))
    coef, still, prev = medium(across, lanes, cells, turned(ghosts), turned(wave_prev), after=[now])
    waves = [prev, now]

    def step(index, head, tail, after):
        left = lax.ppermute(tail, "space", [(i, i + 1) for i in range(spaces - 1)])
        right = lax.ppermute(head, "space", [(i + 1, i) for i in range(spaces - 1)])
        outs = wave_step(
            2.0 * math.cos(1.3 * index), index == STEPS - 1, spot, left, right,
            waves[-1], waves[-2], coef, still, after=after,
        )
        waves.append(outs[0])
        return outs[1:]

    edges = step(0, head, tail, [])
    grads = packed(pack, cuts, me, turned(loglik_grad), after=[waves[-1]])
    grad_parts = [exchange(part, members) for part in grads]
    dist = distances(members, me, cell_parts, after=[waves[-1]])[0]
    dist = jnp.sum(lax.all_gather(dist, "space", axis=0), axis=0)
    edges = step(1, *edges, after=[dist])
    dist = sum(exchange([dist] * members, members))

    moved = []
    order = waves[-1]
    for (low, _), grads in zip(cuts, grad_parts):
        out = updated(members, low, me, dist, cell_parts, grads, after=[order])
        order = out[0]
        moved += exchange(out, members)
    for index in range(2, STEPS):
        edges = step(index, *edges, after=[order])
    ends = [jnp.transpose(wave[..., :across], (2, 0, 1, 3)) for wave in waves[-2:]]
    new_particles = turned(unpacked(pack, cuts, me, moved, after=ends)[0])
    return new_particles, *[jnp.transpose(end, (0, 2, 1, 3)) for end in ends]


def one_cut(pack):
    return [(0, pack.lanes)]


def solution(mesh):
    spec = P("member", None, "space", None)
    return jax.shard_map(
        functools.partial(shards, one_cut),
        mesh=mesh,
        in_specs=(spec, spec, spec, spec, spec, P("member")),
        out_specs=(spec, spec, spec),
        check_vma=False,
    )
```

```python
import functools
import math

import jax
import jax.numpy as jnp
from jax import lax
from jax.experimental import pallas as pl
from jax.experimental.pallas import tpu as pltpu
from jax.sharding import PartitionSpec as P


GHOST = 4
STEPS = 4
LANES = 128

weights = (-205.0 / 72.0, 8.0 / 5.0, -1.0 / 5.0, 8.0 / 315.0, -1.0 / 560.0)
step_size = 0.25
courant = 0.3

VMEM = pl.BlockSpec(memory_space=pltpu.VMEM)
SMEM = pl.BlockSpec(memory_space=pltpu.SMEM)


ANY = pl.BlockSpec(memory_space=pl.ANY)
HBM = pl.BlockSpec(memory_space=pltpu.HBM)


def held(shape, space=pltpu.VMEM):
    return space(tuple(shape), jnp.float32)


def blocks_of(width):
    size = -(-width // 5)
    return [(low, min(low + size, width)) for low in range(0, width, size)]


def call(body, out_shape, in_specs, out_specs, operands, scratch_shapes=(), after=(), near=(), away=()):
    n_in, n_after = len(operands), len(after)
    in_specs, out_specs, operands = list(in_specs), list(out_specs), list(operands)
    scratch = list(scratch_shapes)
    moves = [(i, operands[i]) for i in near] + [(n_in + i, out_shape[i]) for i in away]
    for i, _ in moves:
        if i < n_in:
            in_specs[i] = HBM
            operands[i] = pltpu.with_memory_space_constraint(operands[i], pltpu.HBM)
        else:
            out_specs[i - n_in] = HBM
    if moves:
        blocks = blocks_of(moves[0][1].shape[1])
        scratch += [pltpu.VMEM(array.shape, jnp.float32) for _, array in moves]
        scratch += [pltpu.SemaphoreType.DMA((len(moves), len(blocks)))]

    def ordered(*refs):
        refs = list(refs[:n_in] + refs[n_in + n_after :])
        if not moves:
            return body(*refs)
        refs, stages, sems = refs[: -len(moves) - 1], refs[-len(moves) - 1 : -1], refs[-1]
        coming, leaving = [], []
        for k, (low, high) in enumerate(blocks):
            coming.append([])
            leaving.append([])
            for m, (i, _) in enumerate(moves):
                home, here = refs[i].at[:, low:high], stages[m].at[:, low:high]
                if i < n_in:
                    coming[k].append(pltpu.make_async_copy(home, here, sems.at[m, k]))
                    coming[k][-1].start()
                else:
                    leaving[k].append(pltpu.make_async_copy(here, home, sems.at[m, k]))
        for m, (i, _) in enumerate(moves):
            refs[i] = stages[m]

        def arrive(k):
            for copy in coming[k]:
                copy.wait()

        def leave(k):
            for copy in leaving[k]:
                copy.start()

        body(*refs, arrive=arrive, leave=leave)
        for copies in leaving:
            for copy in copies:
                copy.wait()

    return pl.pallas_call(
        ordered,
        out_shape=out_shape,
        in_specs=in_specs + [ANY] * n_after,
        out_specs=out_specs,
        scratch_shapes=scratch,
        compiler_params=pltpu.CompilerParams(vmem_limit_bytes=26 << 20),
    )(*operands, *after)


class Packing:
    def __init__(self, width, depth, across, members):
        self.width, self.depth, self.across, self.members = width, depth, across, members
        self.rows = width * depth
        self.full = across // LANES
        self.tail = across % LANES
        self.group = LANES // self.tail if self.tail else 1
        self.tail_tiles = -(-self.rows // self.group) if self.tail else 0
        total = self.rows * self.full + self.tail_tiles
        self.tiles = -(-total // members)
        self.lanes = self.tiles * LANES
        self.spare = self.tiles * members - total

    def runs(self, row):
        tile, at, left = row * self.full, 0, self.full
        while left:
            chunk, place = divmod(tile, self.tiles)
            count = min(left, self.tiles - place)
            yield chunk, place * LANES, at * LANES, count * LANES
            tile, at, left = tile + count, at + count, left - count

    def tail_place(self, index):
        chunk, place = divmod(self.rows * self.full + index, self.tiles)
        return chunk, place * LANES


def pack_body(pack, cuts, me_ref, cells_ref, *refs, arrive, leave):
    outs, buf = refs[:-1], refs[-1]
    own = cells_ref.shape[0]
    me = me_ref[0]
    slots = [lax.rem(chunk - me + pack.members, pack.members) for chunk in range(pack.members)]
    starts = {low: k for k, (low, _) in enumerate(blocks_of(pack.width))}
    for row in range(pack.rows):
        x, z = divmod(row, pack.depth)
        if z == 0 and x in starts:
            arrive(starts[x])
        for chunk, there, here, count in pack.runs(row):
            buf[slots[chunk], :, there : there + count] = cells_ref[:, x, z, here : here + count]
    start = pack.full * LANES
    for index in range(pack.tail_tiles):
        chunk, place = pack.tail_place(index)
        pieces = []
        for row in range(index * pack.group, min(pack.rows, (index + 1) * pack.group)):
            x, z = divmod(row, pack.depth)
            pieces.append(cells_ref[:, x, z, start : start + pack.tail])
        empty = LANES - pack.tail * len(pieces)
        if empty:
            pieces.append(jnp.zeros((own, empty), jnp.float32))
        buf[slots[chunk], :, place : place + LANES] = jnp.concatenate(pieces, axis=1)
    for index in range(pack.spare):
        chunk, place = pack.tail_place(pack.tail_tiles + index)
        buf[slots[chunk], :, place : place + LANES] = jnp.zeros((own, LANES), jnp.float32)
    at = 0
    for low, high in cuts:
        for slot in range(pack.members):
            outs[at][...] = buf[slot, :, low:high]
            at += 1


def packed(pack, cuts, me, cells, after=()):
    own = cells.shape[0]
    outs = call(
        functools.partial(pack_body, pack, cuts),
        out_shape=[
            held((own, high - low), pltpu.HBM)
            for low, high in cuts
            for _ in range(pack.members)
        ],
        in_specs=[SMEM, VMEM],
        out_specs=[VMEM] * (len(cuts) * pack.members),
        operands=[me, cells],
        near=(1,),
        scratch_shapes=[pltpu.VMEM((pack.members, own, pack.lanes), jnp.float32)],
        after=after,
    )
    return [outs[i * pack.members : (i + 1) * pack.members] for i in range(len(cuts))]


def unpack_body(pack, cuts, me_ref, *refs, arrive, leave):
    parts, out_ref, buf = refs[:-2], refs[-2], refs[-1]
    me = me_ref[0]
    at = 0
    for low, high in cuts:
        for shift in range(pack.members):
            chunk = lax.rem(me - shift + pack.members, pack.members)
            buf[chunk, :, low:high] = parts[at][...]
            at += 1
    start = pack.full * LANES
    for k, (low, high) in enumerate(blocks_of(pack.width)):
        for row in range(low * pack.depth, high * pack.depth):
            x, z = divmod(row, pack.depth)
            for chunk, there, here, count in pack.runs(row):
                out_ref[:, x, z, here : here + count] = buf[chunk, :, there : there + count]
            if pack.tail:
                chunk, place = pack.tail_place(row // pack.group)
                tile = buf[chunk, :, place : place + LANES]
                at = row % pack.group * pack.tail
                out_ref[:, x, z, start:] = tile[:, at : at + pack.tail]
        leave(k)


def unpacked(pack, cuts, me, parts, after=()):
    own = parts[0].shape[0]
    return call(
        functools.partial(unpack_body, pack, cuts),
        out_shape=[held((own, pack.width, pack.depth, pack.across), pltpu.HBM)],
        in_specs=[SMEM] + [VMEM] * len(parts),
        out_specs=[VMEM],
        operands=[me, *parts],
        scratch_shapes=[pltpu.VMEM((pack.members, own, pack.lanes), jnp.float32)],
        after=after,
        away=(0,),
    )


def distance_body(members, me_ref, *refs):
    parts, out_ref, all_ref = refs[:members], refs[members], refs[members + 1]
    own = parts[0].shape[0]
    me = me_ref[0]
    for shift in range(members):
        row = pl.multiple_of(lax.rem(me - shift + members, members) * own, own)
        all_ref[pl.ds(row, own), :] = parts[shift][...]
    cells = all_ref[...]
    cells = cells - cells[0:1, :]
    gram = lax.dot_general(
        cells,
        cells,
        (((1,), (1,)), ((), ())),
        precision=lax.Precision.HIGHEST,
        preferred_element_type=jnp.float32,
    )
    count = gram.shape[0]
    rows = lax.broadcasted_iota(jnp.int32, (count, count), 0)
    cols = lax.broadcasted_iota(jnp.int32, (count, count), 1)
    diag = jnp.where(rows == cols, gram, 0.0)
    down = jnp.sum(diag, axis=1, keepdims=True)
    along = jnp.sum(diag, axis=0, keepdims=True)
    dist = jnp.where(rows == cols, 0.0, down + along - 2.0 * gram)
    for member in range(members):
        out_ref[:, member * count : (member + 1) * count] = dist[member * own : (member + 1) * own]


def distances(members, me, parts, after=()):
    own, lanes = parts[0].shape
    count = own * members
    return call(
        functools.partial(distance_body, members),
        out_shape=[held((own, members * count))],
        in_specs=[SMEM] + [VMEM] * members,
        out_specs=[VMEM],
        operands=[me, *parts],
        scratch_shapes=[pltpu.VMEM((count, lanes), jnp.float32)],
        after=after,
    )


def add_body(*refs):
    total = refs[0][...]
    for ref in refs[1:-1]:
        total = total + ref[...]
    refs[-1][...] = total


def added(arrays):
    return call(
        add_body, out_shape=[held(arrays[0].shape)], in_specs=[VMEM] * len(arrays), out_specs=[VMEM], operands=arrays
    )


def update_body(members, low, me_ref, dist_ref, *refs):
    cells, grads = refs[:members], refs[members : 2 * members]
    outs = refs[2 * members : 3 * members]
    cell_ref, grad_ref, out_ref = refs[3 * members :]
    own, lanes = grads[0].shape
    count = own * members
    me = me_ref[0]
    for shift in range(members):
        row = pl.multiple_of(lax.rem(me - shift + members, members) * own, own)
        cell_ref[pl.ds(row, own), :] = cells[shift][:, low : low + lanes]
        grad_ref[pl.ds(row, own), :] = grads[shift][...]
    parts = dist_ref[0]
    for index in range(1, dist_ref.shape[0]):
        parts = parts + dist_ref[index]
    dist = jnp.concatenate(
        [parts[:, member * count : (member + 1) * count] for member in range(members)], axis=0
    )
    band = jnp.sum(jnp.sum(dist, axis=1, keepdims=True), axis=0, keepdims=True) / (
        count * (count - 1) * math.log(count + 1)
    )
    kern = jnp.exp(-dist / band)
    total = jnp.sum(kern, axis=1, keepdims=True)
    cell = cell_ref[...]
    mixed = 0.5 * band * grad_ref[...] - cell
    pulled = jnp.dot(
        kern, mixed, precision=lax.Precision.HIGHEST, preferred_element_type=jnp.float32
    )
    out_ref[...] = cell + step_size * (pulled + total * cell)
    for shift in range(members):
        row = pl.multiple_of(lax.rem(me + shift, members) * own, own)
        outs[shift][...] = out_ref[pl.ds(row, own), :]


def updated(members, low, me, dist, cells, grads, after=()):
    own, lanes = grads[0].shape
    count = own * members
    return call(
        functools.partial(update_body, members, low),
        out_shape=[held((own, lanes), pltpu.HBM)] * members,
        in_specs=[SMEM, VMEM] + [VMEM] * (2 * members),
        out_specs=[VMEM] * members,
        operands=[me, dist, *cells, *grads],
        scratch_shapes=[pltpu.VMEM((count, lanes), jnp.float32)] * 3,
        after=after,
    )


def exchange(parts, members):
    return [parts[0]] + [
        lax.ppermute(parts[shift], "member", [(i, (i + shift) % members) for i in range(members)])
        for shift in range(1, members)
    ]


def edges_of(side_ref, cells_ref, inner, outer):
    width, count = cells_ref.shape[0], inner.shape[0]
    side = side_ref[0]
    inner[...] = cells_ref[pl.ds((width - count) * (1 - side), count)]
    outer[...] = cells_ref[pl.ds((width - count) * side, count)]


def between(side_ref, wide, inner_ref, cells_ref, outer_ref):
    width, depth, own, across = cells_ref.shape
    count, lanes = inner_ref.shape[0], wide.shape[-1]
    side = side_ref[0]
    start = (across // LANES) * LANES
    places = ((count + width) * (1 - side), inner_ref), (count, cells_ref), ((count + width) * side, outer_ref)
    for first, part in places:

        def fill(x, carry, first=first, part=part):
            for z in range(depth):
                if lanes > across:
                    wide[first + x, z, :, start:] = jnp.zeros((own, lanes - start), jnp.float32)
                wide[first + x, z, :, :across] = part[x, z]
            return carry

        lax.fori_loop(0, part.shape[0], fill, 0)


def hold_body(side_ref, cells_ref, out_ref, inner_ref, outer_ref, arrive, leave):
    width, depth = out_ref.shape[:2]

    def one(x, carry):
        for z in range(depth):
            out_ref[x, z] = cells_ref[:, x, z, :]
        return carry

    for k, (low, high) in enumerate(blocks_of(width)):
        arrive(k)
        lax.fori_loop(low, high, one, 0)
    edges_of(side_ref, out_ref, inner_ref, outer_ref)


def hold(side, cells, after=()):
    own, width, depth, across = cells.shape
    edge = held((GHOST, depth, own, across))
    return call(
        hold_body,
        out_shape=[held((width, depth, own, across)), edge, edge],
        in_specs=[SMEM, VMEM],
        out_specs=[VMEM] * 3,
        operands=[side, cells],
        near=(1,),
        after=after,
    )


def medium_body(side_ref, cells_ref, ghosts_ref, prev_ref, coef_ref, still_ref, out_ref, inner_ref, outer_ref, arrive, leave):
    own, width, depth, across = cells_ref.shape

    def one(x, carry):
        for z in range(depth):
            out_ref[x, z] = prev_ref[:, x, z, :]
            speed = courant * (1.0 + 0.3 * jnp.tanh(cells_ref[:, x, z, :]))
            coef_ref[x, z] = speed * speed
            total = None
            for offset in range(1, GHOST + 1):
                terms = []
                if z - offset < 0:
                    terms.append(ghosts_ref[:, x, GHOST + z - offset, :])
                if z + offset >= depth:
                    terms.append(ghosts_ref[:, x, GHOST + z + offset - depth, :])
                for term in terms:
                    part = weights[offset] * term
                    total = part if total is None else total + part
            still_ref[x, z] = jnp.zeros((own, across), jnp.float32) if total is None else total
        return carry

    for k, (low, high) in enumerate(blocks_of(width)):
        arrive(k)
        lax.fori_loop(low, high, one, 0)
    for k, ref in enumerate((coef_ref, still_ref)):
        rows = slice(k * GHOST, (k + 1) * GHOST)
        edges_of(side_ref, ref, inner_ref.at[rows], outer_ref.at[rows])


def medium(side, cells, ghosts, prev, after=()):
    own, width, depth, across = cells.shape
    edge = held((2 * GHOST, depth, own, across))
    return call(
        medium_body,
        out_shape=[held((width, depth, own, across))] * 3 + [edge] * 2,
        in_specs=[SMEM] + [VMEM] * 3,
        out_specs=[VMEM] * 5,
        operands=[side, cells, ghosts, prev],
        near=(1, 2, 3),
        after=after,
    )


def sweep(amplitude, across, rows, first, place_ref, source_ref, wide, sums, prev, coef, still, store):
    depth, own, lanes = wide.shape[1:]
    tiles = lanes // LANES
    lane = lax.broadcasted_iota(jnp.int32, (own, LANES), 1)
    particle = lax.broadcasted_iota(jnp.int32, (own, LANES), 0)
    spot = -lane
    for index in range(own):
        cell = source_ref[index] - place_ref[1] * across
        spot = spot + jnp.where(particle == index, cell, 0)

    def tile(t):
        return slice(t * LANES, (t + 1) * LANES)

    def moved(row, t, by):
        up = jnp.where(lane >= by, pltpu.roll(row[t], by, 1), pltpu.roll(row[t - 1], by, 1))
        here, after = row[t], row[(t + 1) % tiles]
        down = jnp.where(
            lane < LANES - by, pltpu.roll(here, LANES - by, 1), pltpu.roll(after, LANES - by, 1)
        )
        return up, down

    def blend(x):
        for z in range(depth):
            row = [wide[x + GHOST, z, :, tile(t)] for t in range(tiles)]
            for t in range(tiles):
                up, down = moved(row, t, 1)
                near, slope = up + down, up - down
                even = (0.5 * (weights[2] + weights[4])) * near + weights[3] * row[t]
                odd = (0.5 * (weights[2] - weights[4])) * slope
                sums[0, x, z, :, tile(t)] = weights[1] * near + (3.0 * weights[0]) * row[t]
                sums[1, x, z, :, tile(t)] = even - odd
                sums[2, x, z, :, tile(t)] = even + odd

    def advance(x):
        for z in range(depth):
            plus = [sums[1, x, z, :, tile(t)] for t in range(tiles)]
            minus = [sums[2, x, z, :, tile(t)] for t in range(tiles)]
            for t in range(tiles):
                count = min(LANES, across - t * LANES)
                if count <= 0:
                    continue
                here = tile(t)
                total = sums[0, x, z, :, here]
                for offset in range(1, GHOST + 1):
                    pair = wide[x + GHOST + offset, z, :, here] + wide[x + GHOST - offset, z, :, here]
                    if z - offset >= 0:
                        pair = pair + wide[x + GHOST, z - offset, :, here]
                    if z + offset < depth:
                        pair = pair + wide[x + GHOST, z + offset, :, here]
                    total = total + weights[offset] * pair
                total = total + (moved(plus, t, 3)[0] + moved(minus, t, 3)[1])
                center, total = wide[x + GHOST, z, :, here][:, :count], total[:, :count]
                there = slice(t * LANES, t * LANES + count)
                total = total + still[x, z, :, there]
                value = 2.0 * center - prev[x, z, :, there] + coef[x, z, :, there] * total
                if z == 0:
                    hit = (spot == (x + first) * across + t * LANES)[:, :count]
                    value = value + jnp.where(hit, amplitude, 0.0)
                store(x, z, there, value)

    def one(x, carry):
        advance(x - 1)
        blend(x)
        return carry

    blend(0)
    lax.fori_loop(1, rows, one, 0)
    advance(rows - 1)


def wave_body(
    amplitude, side_ref, source_ref, inner_ref, outer_ref, now_ref, prev_ref, coef_ref, still_ref,
    out_ref, to_inner_ref, to_outer_ref, wide, sums,
):
    width, _, _, across = now_ref.shape

    def store(x, z, there, value):
        out_ref[x, z, :, there] = value

    between(side_ref, wide, inner_ref, now_ref, outer_ref)
    sweep(amplitude, across, width, 0, side_ref, source_ref, wide, sums, prev_ref, coef_ref, still_ref, store)
    edges_of(side_ref, out_ref, to_inner_ref, to_outer_ref)


def lanes_of(across):
    return -(-(across + GHOST) // LANES) * LANES


def wave_step(amplitude, reach, side, source, edges, now, prev, coef, still, after=()):
    width, depth, own, across = now.shape
    lanes = lanes_of(across)
    return call(
        functools.partial(wave_body, amplitude),
        out_shape=[held(now.shape)] + [held((reach,) + now.shape[1:])] * 2,
        in_specs=[SMEM] * 2 + [VMEM] * 6,
        out_specs=[VMEM] * 3,
        operands=[side, source, *edges, now, prev, coef, still],
        scratch_shapes=[
            pltpu.VMEM((width + 2 * GHOST, depth, own, lanes), jnp.float32),
            pltpu.VMEM((3, width, depth, own, lanes), jnp.float32),
        ],
        after=after,
    )


def last_body(
    amplitudes, side_ref, source_ref, inner_ref, outer_ref, now_ref, before_inner, before_outer, prev_ref,
    medium_inner, medium_outer, coef_ref, still_ref, token_ref, first_ref, second_ref,
    wide, middle, prev, coef, still, sums,
):
    width, depth, own, across = now_ref.shape
    lanes = wide.shape[-1]
    start = (across // LANES) * LANES
    token_ref[...] = jnp.zeros(token_ref.shape, jnp.float32)
    between(side_ref, wide, inner_ref, now_ref, outer_ref)
    between(side_ref, prev, before_inner, prev_ref, before_outer)
    halves = [slice(0, GHOST), slice(GHOST, 2 * GHOST)]
    between(side_ref, coef, medium_inner.at[halves[0]], coef_ref, medium_outer.at[halves[0]])
    between(side_ref, still, medium_inner.at[halves[1]], still_ref, medium_outer.at[halves[1]])

    def clear(x, carry):
        for z in range(depth):
            middle[x, z, :, start:] = jnp.zeros((own, lanes - start), jnp.float32)
        return carry

    lax.fori_loop(0, width + 2 * GHOST, clear, 0)

    def keep(x, z, there, value):
        middle[x, z, :, there] = value

    sweep(amplitudes[0], across, width + 2 * GHOST, -GHOST, side_ref, source_ref, wide, sums, prev, coef, still, keep)

    def turn(x, carry):
        for z in range(depth):
            first_ref[:, x, z, :] = middle[x + GHOST, z, :, :across]
        return carry

    lax.fori_loop(0, width, turn, 0)

    def store(x, z, there, value):
        second_ref[:, x, z, there] = value

    own_rows = wide.at[2 * GHOST : 2 * GHOST + width]
    sweep(amplitudes[1], across, width, 0, side_ref, source_ref, middle, sums, own_rows, coef_ref, still_ref, store)


def last_steps(amplitudes, side, source, edges, now, before, prev, around, coef, still, after=()):
    width, depth, own, across = now.shape
    lanes = lanes_of(across)
    extended = pltpu.VMEM((width + 2 * GHOST, depth, own, lanes), jnp.float32)
    native = held((own, width, depth, across), pltpu.HBM)
    return call(
        functools.partial(last_body, amplitudes),
        out_shape=[held((own, LANES)), native, native],
        in_specs=[SMEM] * 2 + [VMEM] * 10,
        out_specs=[VMEM] * 3,
        operands=[side, source, *edges, now, *before, prev, *around, coef, still],
        scratch_shapes=[
            pltpu.VMEM((width + 4 * GHOST, depth, own, lanes), jnp.float32),
            extended,
            extended,
            extended,
            extended,
            pltpu.VMEM((3, width + 2 * GHOST, depth, own, lanes), jnp.float32),
        ],
        after=after,
    )


def shards(cuts_of, particles, loglik_grad, wave_prev, wave_now, ghosts, src_cell):
    _, depth, width, across = particles.shape
    members = lax.axis_size("member")
    spaces = lax.axis_size("space")
    member_idx = lax.axis_index("member")
    space_idx = lax.axis_index("space")
    pack = Packing(width, depth, across, members)
    whole = [(0, pack.lanes)]
    cuts = cuts_of(pack)
    me = jnp.reshape(member_idx, (1,)).astype(jnp.int32)

    def turned(array):
        return jnp.transpose(array, (0, 2, 1, 3))

    ready = packed(pack, whole, me, turned(particles))[0]
    ready, wave_now = lax.optimization_barrier((ready, wave_now))
    cell_parts = exchange(ready, members)

    side = jnp.stack([space_idx % 2, space_idx * width]).astype(jnp.int32)
    now, inner, outer = hold(side, turned(wave_now))
    coef, still, prev, *around = medium(side, turned(particles), turned(ghosts), turned(wave_prev), after=[now])

    def swap(edge, first):
        pairs = [(i, i + 1) for i in range(first, spaces - 1, 2)]
        return lax.ppermute(edge, "space", pairs + [(j, i) for i, j in pairs])

    def swapped(inner, outer):
        return swap(inner, 0), swap(outer, 1)

    amplitudes = [2.0 * math.cos(1.3 * index) for index in range(STEPS)]
    waves = [prev, now]
    edges = swapped(inner, outer)
    around = swapped(*around)

    def step(index, edges, after=()):
        reach = GHOST if index < STEPS - 3 else 2 * GHOST
        out, inner, outer = wave_step(
            amplitudes[index], reach, side, src_cell, edges, waves[-1], waves[-2], coef, still, after=after
        )
        waves.append(out)
        return swapped(inner, outer)

    before, edges = edges, step(0, edges)
    grads = packed(pack, cuts, me, turned(loglik_grad), after=[waves[-1]])
    grad_parts = []
    for part in grads:
        grad_parts.append(exchange(part, members))
    dist = distances(members, me, cell_parts, after=[waves[2]])[0]
    dist = exchange([dist] * members, members)
    dist = added(dist)[0]
    dist = lax.all_gather(dist, "space", axis=0)
    for index in range(1, STEPS - 2):
        before, edges = edges, step(index, edges, after=[dist])

    moved = []
    order = dist
    for (low, _), grads in zip(cuts, grad_parts):
        out = updated(members, low, me, dist, cell_parts, grads, after=[order])
        order = out[0]
        moved += exchange(out, members)
    token, *ends = last_steps(
        amplitudes[-2:], side, src_cell, edges, waves[-1], before, waves[-2], around, coef, still, after=[order]
    )
    new_particles = unpacked(pack, cuts, me, moved, after=[token])[0]
    return turned(new_particles), turned(ends[0]), turned(ends[1])


def early_cut(pack):
    first = pack.tiles * 1 // 4 * LANES
    return [(0, first), (first, pack.lanes)]


def solution(mesh):
    spec = P("member", None, "space", None)
    return jax.shard_map(
        functools.partial(shards, early_cut),
        mesh=mesh,
        in_specs=(spec, spec, spec, spec, spec, P("member")),
        out_specs=(spec, spec, spec),
        check_vma=False,
    )
```

```python
import functools
import math

import jax
import jax.numpy as jnp
from jax import lax
from jax.experimental import pallas as pl
from jax.experimental.pallas import tpu as pltpu
from jax.sharding import PartitionSpec as P


GHOST = 4
STEPS = 4
LANES = 128

weights = (-205.0 / 72.0, 8.0 / 5.0, -1.0 / 5.0, 8.0 / 315.0, -1.0 / 560.0)
step_size = 0.25
courant = 0.3

VMEM = pl.BlockSpec(memory_space=pltpu.VMEM)
SMEM = pl.BlockSpec(memory_space=pltpu.SMEM)


ANY = pl.BlockSpec(memory_space=pl.ANY)
HBM = pl.BlockSpec(memory_space=pltpu.HBM)


def held(shape, space=pltpu.VMEM):
    return space(tuple(shape), jnp.float32)


def blocks_of(width):
    size = -(-width // 5)
    return [(low, min(low + size, width)) for low in range(0, width, size)]


def call(body, out_shape, in_specs, out_specs, operands, scratch_shapes=(), after=(), near=(), away=()):
    n_in, n_after = len(operands), len(after)
    in_specs, out_specs, operands = list(in_specs), list(out_specs), list(operands)
    scratch = list(scratch_shapes)
    moves = [(i, operands[i]) for i in near] + [(n_in + i, out_shape[i]) for i in away]
    for i, _ in moves:
        if i < n_in:
            in_specs[i] = HBM
            operands[i] = pltpu.with_memory_space_constraint(operands[i], pltpu.HBM)
        else:
            out_specs[i - n_in] = HBM
    if moves:
        blocks = blocks_of(moves[0][1].shape[1])
        scratch += [pltpu.VMEM(array.shape, jnp.float32) for _, array in moves]
        scratch += [pltpu.SemaphoreType.DMA((len(moves), len(blocks)))]

    def ordered(*refs):
        refs = list(refs[:n_in] + refs[n_in + n_after :])
        if not moves:
            return body(*refs)
        refs, stages, sems = refs[: -len(moves) - 1], refs[-len(moves) - 1 : -1], refs[-1]
        coming, leaving = [], []
        for k, (low, high) in enumerate(blocks):
            coming.append([])
            leaving.append([])
            for m, (i, _) in enumerate(moves):
                home, here = refs[i].at[:, low:high], stages[m].at[:, low:high]
                if i < n_in:
                    coming[k].append(pltpu.make_async_copy(home, here, sems.at[m, k]))
                    coming[k][-1].start()
                else:
                    leaving[k].append(pltpu.make_async_copy(here, home, sems.at[m, k]))
        for m, (i, _) in enumerate(moves):
            refs[i] = stages[m]

        def arrive(k):
            for copy in coming[k]:
                copy.wait()

        def leave(k):
            for copy in leaving[k]:
                copy.start()

        body(*refs, arrive=arrive, leave=leave)
        for copies in leaving:
            for copy in copies:
                copy.wait()

    return pl.pallas_call(
        ordered,
        out_shape=out_shape,
        in_specs=in_specs + [ANY] * n_after,
        out_specs=out_specs,
        scratch_shapes=scratch,
        compiler_params=pltpu.CompilerParams(vmem_limit_bytes=26 << 20),
    )(*operands, *after)


class Packing:
    def __init__(self, width, depth, across, members):
        self.width, self.depth, self.across, self.members = width, depth, across, members
        self.rows = width * depth
        self.full = across // LANES
        self.tail = across % LANES
        self.group = LANES // self.tail if self.tail else 1
        self.tail_tiles = -(-self.rows // self.group) if self.tail else 0
        total = self.rows * self.full + self.tail_tiles
        self.tiles = -(-total // members)
        self.lanes = self.tiles * LANES
        self.spare = self.tiles * members - total

    def runs(self, row):
        tile, at, left = row * self.full, 0, self.full
        while left:
            chunk, place = divmod(tile, self.tiles)
            count = min(left, self.tiles - place)
            yield chunk, place * LANES, at * LANES, count * LANES
            tile, at, left = tile + count, at + count, left - count

    def tail_place(self, index):
        chunk, place = divmod(self.rows * self.full + index, self.tiles)
        return chunk, place * LANES


def pack_body(pack, cuts, me_ref, cells_ref, *refs, arrive, leave):
    outs, buf = refs[:-1], refs[-1]
    own = cells_ref.shape[0]
    me = me_ref[0]
    slots = [lax.rem(chunk - me + pack.members, pack.members) for chunk in range(pack.members)]
    starts = {low: k for k, (low, _) in enumerate(blocks_of(pack.width))}
    for row in range(pack.rows):
        x, z = divmod(row, pack.depth)
        if z == 0 and x in starts:
            arrive(starts[x])
        for chunk, there, here, count in pack.runs(row):
            buf[slots[chunk], :, there : there + count] = cells_ref[:, x, z, here : here + count]
    start = pack.full * LANES
    for index in range(pack.tail_tiles):
        chunk, place = pack.tail_place(index)
        pieces = []
        for row in range(index * pack.group, min(pack.rows, (index + 1) * pack.group)):
            x, z = divmod(row, pack.depth)
            pieces.append(cells_ref[:, x, z, start : start + pack.tail])
        empty = LANES - pack.tail * len(pieces)
        if empty:
            pieces.append(jnp.zeros((own, empty), jnp.float32))
        buf[slots[chunk], :, place : place + LANES] = jnp.concatenate(pieces, axis=1)
    for index in range(pack.spare):
        chunk, place = pack.tail_place(pack.tail_tiles + index)
        buf[slots[chunk], :, place : place + LANES] = jnp.zeros((own, LANES), jnp.float32)
    at = 0
    for low, high in cuts:
        for slot in range(pack.members):
            outs[at][...] = buf[slot, :, low:high]
            at += 1


def packed(pack, cuts, me, cells, after=()):
    own = cells.shape[0]
    outs = call(
        functools.partial(pack_body, pack, cuts),
        out_shape=[
            held((own, high - low), pltpu.HBM)
            for low, high in cuts
            for _ in range(pack.members)
        ],
        in_specs=[SMEM, VMEM],
        out_specs=[VMEM] * (len(cuts) * pack.members),
        operands=[me, cells],
        near=(1,),
        scratch_shapes=[pltpu.VMEM((pack.members, own, pack.lanes), jnp.float32)],
        after=after,
    )
    return [outs[i * pack.members : (i + 1) * pack.members] for i in range(len(cuts))]


def unpack_body(pack, cuts, me_ref, *refs, arrive, leave):
    parts, out_ref, buf = refs[:-2], refs[-2], refs[-1]
    me = me_ref[0]
    at = 0
    for low, high in cuts:
        for shift in range(pack.members):
            chunk = lax.rem(me - shift + pack.members, pack.members)
            buf[chunk, :, low:high] = parts[at][...]
            at += 1
    start = pack.full * LANES
    for k, (low, high) in enumerate(blocks_of(pack.width)):
        for row in range(low * pack.depth, high * pack.depth):
            x, z = divmod(row, pack.depth)
            for chunk, there, here, count in pack.runs(row):
                out_ref[:, x, z, here : here + count] = buf[chunk, :, there : there + count]
            if pack.tail:
                chunk, place = pack.tail_place(row // pack.group)
                tile = buf[chunk, :, place : place + LANES]
                at = row % pack.group * pack.tail
                out_ref[:, x, z, start:] = tile[:, at : at + pack.tail]
        leave(k)


def unpacked(pack, cuts, me, parts, after=()):
    own = parts[0].shape[0]
    return call(
        functools.partial(unpack_body, pack, cuts),
        out_shape=[held((own, pack.width, pack.depth, pack.across), pltpu.HBM)],
        in_specs=[SMEM] + [VMEM] * len(parts),
        out_specs=[VMEM],
        operands=[me, *parts],
        scratch_shapes=[pltpu.VMEM((pack.members, own, pack.lanes), jnp.float32)],
        after=after,
        away=(0,),
    )


def distance_body(members, me_ref, *refs):
    parts, out_ref, all_ref = refs[:members], refs[members], refs[members + 1]
    own = parts[0].shape[0]
    me = me_ref[0]
    for shift in range(members):
        row = pl.multiple_of(lax.rem(me - shift + members, members) * own, own)
        all_ref[pl.ds(row, own), :] = parts[shift][...]
    cells = all_ref[...]
    cells = cells - cells[0:1, :]
    gram = lax.dot_general(
        cells,
        cells,
        (((1,), (1,)), ((), ())),
        precision=lax.Precision.HIGHEST,
        preferred_element_type=jnp.float32,
    )
    count = gram.shape[0]
    rows = lax.broadcasted_iota(jnp.int32, (count, count), 0)
    cols = lax.broadcasted_iota(jnp.int32, (count, count), 1)
    diag = jnp.where(rows == cols, gram, 0.0)
    down = jnp.sum(diag, axis=1, keepdims=True)
    along = jnp.sum(diag, axis=0, keepdims=True)
    dist = jnp.where(rows == cols, 0.0, down + along - 2.0 * gram)
    for member in range(members):
        out_ref[:, member * count : (member + 1) * count] = dist[member * own : (member + 1) * own]


def distances(members, me, parts, after=()):
    own, lanes = parts[0].shape
    count = own * members
    return call(
        functools.partial(distance_body, members),
        out_shape=[held((own, members * count))],
        in_specs=[SMEM] + [VMEM] * members,
        out_specs=[VMEM],
        operands=[me, *parts],
        scratch_shapes=[pltpu.VMEM((count, lanes), jnp.float32)],
        after=after,
    )


def add_body(*refs):
    total = refs[0][...]
    for ref in refs[1:-1]:
        total = total + ref[...]
    refs[-1][...] = total


def added(arrays):
    return call(
        add_body, out_shape=[held(arrays[0].shape)], in_specs=[VMEM] * len(arrays), out_specs=[VMEM], operands=arrays
    )


def update_body(members, low, me_ref, dist_ref, *refs):
    cells, grads = refs[:members], refs[members : 2 * members]
    outs = refs[2 * members : 3 * members]
    cell_ref, grad_ref, out_ref = refs[3 * members :]
    own, lanes = grads[0].shape
    count = own * members
    me = me_ref[0]
    for shift in range(members):
        row = pl.multiple_of(lax.rem(me - shift + members, members) * own, own)
        cell_ref[pl.ds(row, own), :] = cells[shift][:, low : low + lanes]
        grad_ref[pl.ds(row, own), :] = grads[shift][...]
    parts = dist_ref[0]
    for index in range(1, dist_ref.shape[0]):
        parts = parts + dist_ref[index]
    dist = jnp.concatenate(
        [parts[:, member * count : (member + 1) * count] for member in range(members)], axis=0
    )
    band = jnp.sum(jnp.sum(dist, axis=1, keepdims=True), axis=0, keepdims=True) / (
        count * (count - 1) * math.log(count + 1)
    )
    kern = jnp.exp(-dist / band)
    total = jnp.sum(kern, axis=1, keepdims=True)
    cell = cell_ref[...]
    mixed = 0.5 * band * grad_ref[...] - cell
    pulled = jnp.dot(
        kern, mixed, precision=lax.Precision.HIGHEST, preferred_element_type=jnp.float32
    )
    out_ref[...] = cell + step_size * (pulled + total * cell)
    for shift in range(members):
        row = pl.multiple_of(lax.rem(me + shift, members) * own, own)
        outs[shift][...] = out_ref[pl.ds(row, own), :]


def updated(members, low, me, dist, cells, grads, after=()):
    own, lanes = grads[0].shape
    count = own * members
    return call(
        functools.partial(update_body, members, low),
        out_shape=[held((own, lanes), pltpu.HBM)] * members,
        in_specs=[SMEM, VMEM] + [VMEM] * (2 * members),
        out_specs=[VMEM] * members,
        operands=[me, dist, *cells, *grads],
        scratch_shapes=[pltpu.VMEM((count, lanes), jnp.float32)] * 3,
        after=after,
    )


def exchange(parts, members):
    return [parts[0]] + [
        lax.ppermute(parts[shift], "member", [(i, (i + shift) % members) for i in range(members)])
        for shift in range(1, members)
    ]


def edges_of(side_ref, cells_ref, inner, outer):
    width, count = cells_ref.shape[0], inner.shape[0]
    side = side_ref[0]
    inner[...] = cells_ref[pl.ds((width - count) * (1 - side), count)]
    outer[...] = cells_ref[pl.ds((width - count) * side, count)]


def between(side_ref, wide, inner_ref, cells_ref, outer_ref):
    width, depth, own, across = cells_ref.shape
    count, lanes = inner_ref.shape[0], wide.shape[-1]
    side = side_ref[0]
    start = (across // LANES) * LANES
    places = ((count + width) * (1 - side), inner_ref), (count, cells_ref), ((count + width) * side, outer_ref)
    for first, part in places:

        def fill(x, carry, first=first, part=part):
            for z in range(depth):
                if lanes > across:
                    wide[first + x, z, :, start:] = jnp.zeros((own, lanes - start), jnp.float32)
                wide[first + x, z, :, :across] = part[x, z]
            return carry

        lax.fori_loop(0, part.shape[0], fill, 0)


def hold_body(side_ref, cells_ref, out_ref, inner_ref, outer_ref, arrive, leave):
    width, depth = out_ref.shape[:2]

    def one(x, carry):
        for z in range(depth):
            out_ref[x, z] = cells_ref[:, x, z, :]
        return carry

    for k, (low, high) in enumerate(blocks_of(width)):
        arrive(k)
        lax.fori_loop(low, high, one, 0)
    edges_of(side_ref, out_ref, inner_ref, outer_ref)


def hold(side, cells, after=()):
    own, width, depth, across = cells.shape
    edge = held((GHOST, depth, own, across))
    return call(
        hold_body,
        out_shape=[held((width, depth, own, across)), edge, edge],
        in_specs=[SMEM, VMEM],
        out_specs=[VMEM] * 3,
        operands=[side, cells],
        near=(1,),
        after=after,
    )


def medium_body(cells_ref, ghosts_ref, prev_ref, coef_ref, still_ref, out_ref, arrive, leave):
    own, width, depth, across = cells_ref.shape

    def one(x, carry):
        for z in range(depth):
            out_ref[x, z] = prev_ref[:, x, z, :]
            speed = courant * (1.0 + 0.3 * jnp.tanh(cells_ref[:, x, z, :]))
            coef_ref[x, z] = speed * speed
            total = None
            for offset in range(1, GHOST + 1):
                terms = []
                if z - offset < 0:
                    terms.append(ghosts_ref[:, x, GHOST + z - offset, :])
                if z + offset >= depth:
                    terms.append(ghosts_ref[:, x, GHOST + z + offset - depth, :])
                for term in terms:
                    part = weights[offset] * term
                    total = part if total is None else total + part
            still_ref[x, z] = jnp.zeros((own, across), jnp.float32) if total is None else total
        return carry

    for k, (low, high) in enumerate(blocks_of(width)):
        arrive(k)
        lax.fori_loop(low, high, one, 0)


def medium(cells, ghosts, prev, after=()):
    own, width, depth, across = cells.shape
    return call(
        medium_body,
        out_shape=[held((width, depth, own, across))] * 3,
        in_specs=[VMEM] * 3,
        out_specs=[VMEM] * 3,
        operands=[cells, ghosts, prev],
        near=(0, 1, 2),
        after=after,
    )


def sweep(amplitude, across, rows, first, place_ref, source_ref, wide, sums, prev, coef, still, store):
    depth, own, lanes = wide.shape[1:]
    tiles = lanes // LANES
    lane = lax.broadcasted_iota(jnp.int32, (own, LANES), 1)
    particle = lax.broadcasted_iota(jnp.int32, (own, LANES), 0)
    spot = -lane
    for index in range(own):
        cell = source_ref[index] - place_ref[1] * across
        spot = spot + jnp.where(particle == index, cell, 0)

    def tile(t):
        return slice(t * LANES, (t + 1) * LANES)

    def moved(row, t, by):
        up = jnp.where(lane >= by, pltpu.roll(row[t], by, 1), pltpu.roll(row[t - 1], by, 1))
        here, after = row[t], row[(t + 1) % tiles]
        down = jnp.where(
            lane < LANES - by, pltpu.roll(here, LANES - by, 1), pltpu.roll(after, LANES - by, 1)
        )
        return up, down

    def blend(x):
        for z in range(depth):
            row = [wide[x + GHOST, z, :, tile(t)] for t in range(tiles)]
            for t in range(tiles):
                up, down = moved(row, t, 1)
                near, slope = up + down, up - down
                even = (0.5 * (weights[2] + weights[4])) * near + weights[3] * row[t]
                odd = (0.5 * (weights[2] - weights[4])) * slope
                sums[0, x & 1, z, :, tile(t)] = weights[1] * near + (3.0 * weights[0]) * row[t]
                sums[1, x & 1, z, :, tile(t)] = even - odd
                sums[2, x & 1, z, :, tile(t)] = even + odd

    def advance(x):
        for z in range(depth):
            plus = [sums[1, x & 1, z, :, tile(t)] for t in range(tiles)]
            minus = [sums[2, x & 1, z, :, tile(t)] for t in range(tiles)]
            for t in range(tiles):
                count = min(LANES, across - t * LANES)
                if count <= 0:
                    continue
                here = tile(t)
                total = sums[0, x & 1, z, :, here]
                for offset in range(1, GHOST + 1):
                    pair = wide[x + GHOST + offset, z, :, here] + wide[x + GHOST - offset, z, :, here]
                    if z - offset >= 0:
                        pair = pair + wide[x + GHOST, z - offset, :, here]
                    if z + offset < depth:
                        pair = pair + wide[x + GHOST, z + offset, :, here]
                    total = total + weights[offset] * pair
                total = total + (moved(plus, t, 3)[0] + moved(minus, t, 3)[1])
                center, total = wide[x + GHOST, z, :, here][:, :count], total[:, :count]
                there = slice(t * LANES, t * LANES + count)
                total = total + still[x, z, :, there]
                value = 2.0 * center - prev[x, z, :, there] + coef[x, z, :, there] * total
                if z == 0:
                    hit = (spot == (x + first) * across + t * LANES)[:, :count]
                    value = value + jnp.where(hit, amplitude, 0.0)
                store(x, z, there, value)

    def one(x, carry):
        advance(x - 1)
        blend(x)
        return carry

    blend(0)
    lax.fori_loop(1, rows, one, 0)
    advance(rows - 1)


def wave_body(
    amplitude, reach, side_ref, source_ref, inner_ref, outer_ref, now_ref, prev_ref, coef_ref, still_ref,
    out_ref, to_inner_ref, to_outer_ref, wide, sums,
):
    width, _, _, across = now_ref.shape

    def store(x, z, there, value):
        out_ref[x, z, :, there] = value

    between(side_ref, wide, inner_ref.at[0:GHOST], now_ref, outer_ref.at[0:GHOST])
    sweep(amplitude, across, width, 0, side_ref, source_ref, wide, sums, prev_ref, coef_ref, still_ref, store)
    low = 0
    for count, ref in zip(reach, (out_ref, coef_ref, still_ref)):
        rows = slice(low, low + count)
        edges_of(side_ref, ref, to_inner_ref.at[rows], to_outer_ref.at[rows])
        low += count


def lanes_of(across):
    return -(-(across + GHOST) // LANES) * LANES


def wave_step(amplitude, reach, side, source, edges, now, prev, coef, still, after=()):
    width, depth, own, across = now.shape
    lanes = lanes_of(across)
    return call(
        functools.partial(wave_body, amplitude, reach),
        out_shape=[held(now.shape)] + [held((sum(reach),) + now.shape[1:])] * 2,
        in_specs=[SMEM] * 2 + [VMEM] * 6,
        out_specs=[VMEM] * 3,
        operands=[side, source, *edges, now, prev, coef, still],
        scratch_shapes=[
            pltpu.VMEM((width + 2 * GHOST, depth, own, lanes), jnp.float32),
            pltpu.VMEM((3, 2, depth, own, lanes), jnp.float32),
        ],
        after=after,
    )


def last_body(
    amplitudes, side_ref, source_ref, inner_ref, outer_ref, now_ref, before_inner, before_outer, prev_ref,
    coef_ref, still_ref, token_ref, first_ref, second_ref,
    wide, middle, prev, coef, still, sums,
):
    width, depth, own, across = now_ref.shape
    lanes = wide.shape[-1]
    start = (across // LANES) * LANES
    token_ref[...] = jnp.zeros(token_ref.shape, jnp.float32)
    between(side_ref, wide, inner_ref, now_ref, outer_ref)
    for k, (part, ref) in enumerate(((prev, prev_ref), (coef, coef_ref), (still, still_ref))):
        rows = slice(k * GHOST, (k + 1) * GHOST)
        between(side_ref, part, before_inner.at[rows], ref, before_outer.at[rows])

    def clear(x, carry):
        for z in range(depth):
            middle[x, z, :, start:] = jnp.zeros((own, lanes - start), jnp.float32)
        return carry

    lax.fori_loop(0, width + 2 * GHOST, clear, 0)

    def keep(x, z, there, value):
        middle[x, z, :, there] = value

    sweep(amplitudes[0], across, width + 2 * GHOST, -GHOST, side_ref, source_ref, wide, sums, prev, coef, still, keep)

    def turn(x, carry):
        for z in range(depth):
            first_ref[:, x, z, :] = middle[x + GHOST, z, :, :across]
        return carry

    lax.fori_loop(0, width, turn, 0)

    def store(x, z, there, value):
        second_ref[:, x, z, there] = value

    own_rows = wide.at[2 * GHOST : 2 * GHOST + width]
    sweep(amplitudes[1], across, width, 0, side_ref, source_ref, middle, sums, own_rows, coef_ref, still_ref, store)


def last_steps(amplitudes, side, source, edges, now, before, prev, coef, still, after=()):
    width, depth, own, across = now.shape
    lanes = lanes_of(across)
    extended = pltpu.VMEM((width + 2 * GHOST, depth, own, lanes), jnp.float32)
    native = held((own, width, depth, across), pltpu.HBM)
    return call(
        functools.partial(last_body, amplitudes),
        out_shape=[held((own, LANES)), native, native],
        in_specs=[SMEM] * 2 + [VMEM] * 8,
        out_specs=[VMEM] * 3,
        operands=[side, source, *edges, now, *before, prev, coef, still],
        scratch_shapes=[
            pltpu.VMEM((width + 4 * GHOST, depth, own, lanes), jnp.float32),
            extended,
            extended,
            extended,
            extended,
            pltpu.VMEM((3, 2, depth, own, lanes), jnp.float32),
        ],
        after=after,
    )


def shards(cuts_of, particles, loglik_grad, wave_prev, wave_now, ghosts, src_cell):
    _, depth, width, across = particles.shape
    members = lax.axis_size("member")
    spaces = lax.axis_size("space")
    member_idx = lax.axis_index("member")
    space_idx = lax.axis_index("space")
    pack = Packing(width, depth, across, members)
    whole = [(0, pack.lanes)]
    cuts = cuts_of(pack)
    me = jnp.reshape(member_idx, (1,)).astype(jnp.int32)

    def turned(array):
        return jnp.transpose(array, (0, 2, 1, 3))

    ready = packed(pack, whole, me, turned(particles))[0]
    ready, wave_now = lax.optimization_barrier((ready, wave_now))
    cell_parts = exchange(ready, members)

    side = jnp.stack([space_idx % 2, space_idx * width]).astype(jnp.int32)
    now, inner, outer = hold(side, turned(wave_now))
    coef, still, prev = medium(turned(particles), turned(ghosts), turned(wave_prev), after=[now])

    def swap(edge, first):
        pairs = [(i, i + 1) for i in range(first, spaces - 1, 2)]
        return lax.ppermute(edge, "space", pairs + [(j, i) for i, j in pairs])

    def swapped(inner, outer):
        return swap(inner, 0), swap(outer, 1)

    amplitudes = [2.0 * math.cos(1.3 * index) for index in range(STEPS)]
    waves = [prev, now]
    edges = swapped(inner, outer)

    def step(index, edges, after=()):
        reach = (2 * GHOST,) if index == STEPS - 3 else (GHOST,) * (3 if index == STEPS - 4 else 1)
        out, inner, outer = wave_step(
            amplitudes[index], reach, side, src_cell, edges, waves[-1], waves[-2], coef, still, after=after
        )
        waves.append(out)
        return swapped(inner, outer)

    before, edges = edges, step(0, edges)
    grads = packed(pack, cuts, me, turned(loglik_grad), after=[waves[-1]])
    grad_parts = []
    for part in grads:
        grad_parts.append(exchange(part, members))
    dist = distances(members, me, cell_parts, after=[waves[2]])[0]
    dist = exchange([dist] * members, members)
    dist = added(dist)[0]
    dist = lax.all_gather(dist, "space", axis=0)
    for index in range(1, STEPS - 2):
        before, edges = edges, step(index, edges, after=[dist])

    moved = []
    order = dist
    for (low, _), grads in zip(cuts, grad_parts):
        out = updated(members, low, me, dist, cell_parts, grads, after=[order])
        order = out[0]
        moved += exchange(out, members)
    token, *ends = last_steps(
        amplitudes[-2:], side, src_cell, edges, waves[-1], before, waves[-2], coef, still, after=[order]
    )
    new_particles = unpacked(pack, cuts, me, moved, after=[token])[0]
    return turned(new_particles), turned(ends[0]), turned(ends[1])


def early_cut(pack):
    first = pack.tiles * 1 // 4 * LANES
    return [(0, first), (first, pack.lanes)]


def solution(mesh):
    spec = P("member", None, "space", None)
    return jax.shard_map(
        functools.partial(shards, early_cut),
        mesh=mesh,
        in_specs=(spec, spec, spec, spec, spec, P("member")),
        out_specs=(spec, spec, spec),
        check_vma=False,
    )
```
